256 devices in a mesh: modes: 64 (over y, x, z_hi), mom: 4 (over z_lo, core).
Axes of the slice: x: 4, y: 4, z: 8 (z_hi: 4, z_lo: 2; z = z_hi * 2 + z_lo), core: 2. Of those that a mesh axis runs over, the one named last changes fastest.
Arguments:
- elementals: float32 [2, 8, 256, 256, 256], P(None, 'mom', 'modes'), parts along dimension 1, may hold values from -64 to 64
- perambulators: float32 [64, 2, 2, 256, 256], P('modes'), may hold values from -0.25 to 0.25
- owners: int32 [2], replicated, may hold values from 0 to 63
- pairing: int32 [8], P('mom'), parts along dimension 0, may hold values from 0 to 1
Outputs:
- propagated: bfloat16 [2, 8, 2, 256, 256, 256], P(None, 'mom', None, 'modes'), parts along dimension 1
- correlator: float32 [2, 8, 2], P(None, 'mom'), parts along dimension 1
The draws below stay inside these ranges and needn't reach their ends.
There are 4 independent parts, one for each index of `mom`. The reference program is written for one: setup_inputs(seed, part) draws one part's arguments, and reference() takes and returns one part's arrays. A program takes and returns all parts, laid end to end along the dimension named above; an argument that names none is the same for every part. Nothing has to cross between parts.
All inputs are finite; a program needn't handle non-finite values.
Results may differ from the reference program's by a relative error of at most 0.001.
Values sent between devices are 32-bit elements; how exact they have to be, the bound alone decides.
No kernel may reach another device: no remote copies, remote signals or barrier semaphores. Data moves between devices by JAX's collectives and lax.ppermute only.
A program may use at most 128 MiB of HBM per device.

```python
import jax
import jax.numpy as jnp
from jax import lax

N = 256
MOMS = 2
TIMES = 2
N_MODES = 64


def draw_elementals(key, part):
    base_key = jax.random.fold_in(jax.random.fold_in(key, 17), 0)
    full_shape = (2, MOMS, N, N, N)
    position_ramp = jnp.arange(N, dtype=jnp.float32) / max(N - 1, 1)
    values = jax.random.truncated_normal(base_key, -6.0, 6.0, full_shape, jnp.float32)
    rising = jnp.exp(jnp.log(3.0) * position_ramp)
    return values * rising[None, None, :, None, None]


def level_of(stream_key, extent, shards, smallest, top_value):
    factor_of, own = 1.0, jax.random.fold_in(stream_key, 6)
    for dim, blocks in shards:
        draws = jnp.exp(jax.random.uniform(jax.random.fold_in(own, dim), (blocks,), jnp.float32, smallest / len(shards), top_value / len(shards)))
        factor_of = factor_of * jnp.repeat(draws, extent[dim] // blocks).reshape([-1 if axis == dim else 1 for axis in range(len(extent))])
    return factor_of


def centred(key, extent, scale, reach, shards=(), held_as=jnp.bfloat16):
    result = jax.random.normal(key, extent, jnp.float32) * scale
    if len(shards) > 0:
        result = level_of(key, extent, shards, -0.22, 0.18) * result
    return jnp.clip(result, min=-reach, max=reach).astype(held_as)


def setup_inputs(seed: int = 0, part: int = 0) -> dict:
    arg_keys = jax.random.split(jax.random.key(seed), 5)
    part_splits = jax.random.split(jax.random.fold_in(arg_keys[4], part), 5)
    return {
        "elementals": draw_elementals(jax.random.fold_in(jax.random.fold_in(arg_keys[4], part), 71), part),
        "perambulators": centred(arg_keys[1], (N_MODES, TIMES, 2, N, N), (2 * N) ** -0.5, 0.25, ((0, 64),), jnp.float32),
        "owners": jax.random.randint(arg_keys[2], (TIMES,), 0, N_MODES).astype(jnp.int32),
        "pairing": jax.random.randint(part_splits[3], (MOMS,), 0, MOMS).astype(jnp.int32),
    }


highest = lax.Precision.HIGHEST


def complex_product(formula, matrix_re, matrix_im, tensor_re, tensor_im):
    def single(left_part, right_part):
        return jnp.einsum(formula, left_part, right_part, precision=highest)
    real_part = single(matrix_re, tensor_re) - single(matrix_im, tensor_im)
    imag_part = single(matrix_re, tensor_im) + single(matrix_im, tensor_re)
    return real_part, imag_part


def transform(elem_re, elem_im, peram_re, peram_im):
    third_re, third_im = complex_product("kc,abc->abk", peram_re, peram_im, elem_re, elem_im)
    second_re, second_im = complex_product("jb,abk->kaj", peram_re, peram_im, third_re, third_im)
    return complex_product("ia,kaj->kij", peram_re, peram_im, second_re, second_im)


def reference(elementals, perambulators, owners, pairing):
    norm_scale = float(N) ** -1.5
    sink_slabs = []
    for mom_index in range(MOMS):
        picked = lax.dynamic_index_in_dim(elementals, pairing[mom_index], 1, keepdims=False)
        sink_slabs.append((jnp.swapaxes(picked[0], 1, 2), jnp.swapaxes(picked[1], 1, 2)))
    real_rows = []
    imag_rows = []
    corr_real = []
    corr_imag = []
    for mom_index in range(MOMS):
        time_real = []
        time_imag = []
        sums_real = []
        sums_imag = []
        for time_index in range(TIMES):
            peram_now = lax.dynamic_index_in_dim(perambulators[:, time_index], owners[time_index], 0, keepdims=False)
            out_re, out_im = transform(elementals[0, mom_index], elementals[1, mom_index], peram_now[0], peram_now[1])
            sink_re, sink_im = sink_slabs[mom_index]
            sums_real.append(jnp.sum(sink_re * out_re + sink_im * out_im) * norm_scale)
            sums_imag.append(jnp.sum(sink_re * out_im - sink_im * out_re) * norm_scale)
            time_real.append(out_re)
            time_imag.append(out_im)
        real_rows.append(jnp.stack(time_real))
        imag_rows.append(jnp.stack(time_imag))
        corr_real.append(jnp.stack(sums_real))
        corr_imag.append(jnp.stack(sums_imag))
    propagated = jnp.stack([jnp.stack(real_rows), jnp.stack(imag_rows)]).astype(jnp.bfloat16)
    correlator = jnp.stack([jnp.stack(corr_real), jnp.stack(corr_imag)])
    return propagated, correlator
```

```python
import jax
import jax.numpy as jnp
from jax import lax
from jax.experimental import pallas as pl
from jax.experimental.pallas import tpu as pltpu
from jax.sharding import PartitionSpec as P

N = 256
ROWS = 64
MOMS = 2
TIMES = 2
F32 = jnp.float32
BF16 = jnp.bfloat16
VMEM = pl.BlockSpec(memory_space=pltpu.VMEM)
SMEM = pl.BlockSpec(memory_space=pltpu.SMEM)
ANY = pl.BlockSpec(memory_space=pl.ANY)


def halves(x):
    high = x.astype(BF16)
    return high, (x - high.astype(F32)).astype(BF16)


def dot(a, b):
    return jnp.dot(a, b, preferred_element_type=F32)


def dot3(a, b):
    return dot(a[0], b[0]) + (dot(a[0], b[1]) + dot(a[1], b[0]))


def call(body, outs, scratch, limit, flops, nbytes, specs, aliases=None):
    return pl.pallas_call(
        body,
        out_shape=[jax.ShapeDtypeStruct(shape, dtype) for shape, dtype, _ in outs],
        in_specs=specs,
        out_specs=[spec for _, _, spec in outs],
        scratch_shapes=scratch,
        input_output_aliases=aliases or {},
        compiler_params=pltpu.CompilerParams(vmem_limit_bytes=limit << 20),
        cost_estimate=pl.CostEstimate(flops=flops, bytes_accessed=nbytes, transcendentals=0),
    )


def turn_body(elem_ref, high_ref, low_ref):
    for comp in range(2):
        high, low = halves(elem_ref[comp, 0, 0].T)
        high_ref[0, 0, comp * N : (comp + 1) * N, :] = high
        low_ref[0, 0, comp * N : (comp + 1) * N, :] = low


def turn(elementals):
    slab = elementals.shape[2]
    out = jax.ShapeDtypeStruct((MOMS, slab, 2 * N, N), BF16)
    spec = pl.BlockSpec((1, 1, 2 * N, N), lambda m, a: (m, a, 0, 0))
    return pl.pallas_call(
        turn_body,
        grid=(MOMS, slab),
        out_shape=[out, out],
        in_specs=[pl.BlockSpec((2, 1, 1, N, N), lambda m, a: (0, m, a, 0, 0))],
        out_specs=[spec, spec],
        compiler_params=pltpu.CompilerParams(vmem_limit_bytes=16 << 20),
        cost_estimate=pl.CostEstimate(flops=1 << 20, bytes_accessed=8 << 20, transcendentals=0),
    )(elementals)


def first_body(peram_ref, high_ref, low_ref, send_ref, wh_ref, wl_ref):
    for time in range(TIMES):
        re = peram_ref[2 * time]
        im = peram_ref[2 * time + 1]
        for comp, left, right in ((0, re, -im), (1, im, re)):
            rows = pl.ds((2 * time + comp) * ROWS, ROWS)
            for col, part in ((0, left), (N, right)):
                high, low = halves(part)
                wh_ref[rows, col : col + N] = high
                wl_ref[rows, col : col + N] = low

    def step(index, carry):
        mom = index // 4
        a = index % 4
        product = dot3(
            (wh_ref[...], wl_ref[...]), (high_ref[mom, a], low_ref[mom, a])
        )
        for time in range(TIMES):
            for comp in range(2):
                row = (2 * time + comp) * ROWS
                for half in range(2):
                    start = ((mom * TIMES + time) * 2 + half) * 8 + comp * 4 + a
                    send_ref[pl.ds(start, ROWS, stride=64), :] = product[
                        row : row + ROWS, half * 128 : (half + 1) * 128
                    ]
        return carry

    lax.fori_loop(0, 2 * 4, step, 0)


def first(peram, high, low):
    (send,) = call(
        first_body,
        [((ROWS * 64, 128), F32, VMEM)],
        [pltpu.VMEM((4 * ROWS, 2 * N), BF16)] * 2,
        8,
        3 * 2 * 256 * 512 * 256 * 8,
        6 << 20,
        [VMEM] * 3,
    )(peram, high, low)
    return send.reshape(64, 64, 128)


def weights_body(quarter_ref, own_ref, g1_ref, g2_ref, g3_ref, vh_ref, vl_ref, wh_ref, wl_ref):
    quarter = quarter_ref[0]
    nat = lax.broadcasted_iota(jnp.int32, (N, N), 0)
    col = lax.broadcasted_iota(jnp.int32, (N, N), 1)
    place = 4 * (col & 63) + ((quarter + (col >> 6)) & 3)
    order = (nat == place).astype(F32).astype(BF16)
    row = lax.broadcasted_iota(jnp.int32, (2 * N, 2 * N), 0)
    col = lax.broadcasted_iota(jnp.int32, (2 * N, 2 * N), 1)
    place = N * ((col >> 2) & 1) + 4 * (col >> 3) + (col & 3)
    spread = (row == place).astype(F32).astype(BF16)
    for time in range(TIMES):
        parts = []
        for comp in range(2):
            index = 2 * time + comp
            stacked = jnp.concatenate(
                [ref[index] for ref in (own_ref, g1_ref, g2_ref, g3_ref)], axis=0
            )
            parts.append([dot(order, part) for part in halves(stacked)])
        for which, v_ref, w_ref in ((0, vh_ref, wh_ref), (1, vl_ref, wl_ref)):
            re = parts[0][which]
            im = parts[1][which]
            re_t = re.T.astype(BF16)
            im_t = im.T
            v_ref[time, :N, :N] = re_t
            v_ref[time, :N, N:] = im_t.astype(BF16)
            v_ref[time, N:, :N] = (-im_t).astype(BF16)
            v_ref[time, N:, N:] = re_t
            re = re.astype(BF16)
            minus = (-im).astype(BF16)
            im = im.astype(BF16)
            w_ref[time, :N] = (dot(re, spread[:N]) + dot(minus, spread[N:])).astype(BF16)
            w_ref[time, N:] = (dot(im, spread[:N]) + dot(re, spread[N:])).astype(BF16)


def weights(quarter, pieces):
    shape = ((TIMES, 2 * N, 2 * N), BF16, VMEM)
    return call(
        weights_body,
        [shape] * 4,
        [],
        16,
        2 * 2 * 2 * 2 * 256 * 512 * 512,
        5 << 20,
        [SMEM] + [VMEM] * 4,
    )(quarter, *pieces)


def last_body(
    row_ref, pair_ref, got_ref, vh_ref, vl_ref, wh_ref, wl_ref, high_ref, low_ref, sums_ref, old_ref,
    out_ref, total_ref, held, sems,
):
    del old_ref
    row = row_ref[0]
    lane = lax.broadcasted_iota(jnp.int32, (64, 128), 1)

    def copies(index):
        mom, time = index // TIMES, index % TIMES
        return [
            pltpu.make_async_copy(
                held.at[index, comp], out_ref.at[comp, mom, time, row], sems.at[index, comp]
            )
            for comp in range(2)
        ]

    def step(index, totals):
        mom, time = index // TIMES, index % TIMES
        got = jnp.concatenate(
            [
                got_ref[:, pl.ds(pl.multiple_of((index * 2 + half) * 8, 8), 8), :].reshape(512, 128)
                for half in range(2)
            ],
            axis=1,
        )
        first_two = dot3((wh_ref[time], wl_ref[time]), halves(got))
        high, low = halves(first_two)
        full = dot3((high[:N], low[:N]), (vh_ref[time, :N], vl_ref[time, :N])) + dot3(
            (high[N:], low[N:]), (vh_ref[time, N:], vl_ref[time, N:])
        )
        re, im = full[:, :N], full[:, N:]
        held[index, 0] = re.astype(BF16)
        held[index, 1] = im.astype(BF16)
        for copy in copies(index):
            copy.start()
        pair = pair_ref[mom]
        sink = high_ref[pair, row].astype(F32) + low_ref[pair, row].astype(F32)
        sink_re, sink_im = sink[:N], sink[N:]
        real = jnp.sum(sink_re * re + sink_im * im)
        imag = jnp.sum(sink_re * im - sink_im * re)
        totals = totals + jnp.where(lane == index, real, 0.0)
        return totals + jnp.where(lane == index + 4, imag, 0.0)

    total_ref[...] = lax.fori_loop(0, MOMS * TIMES, step, sums_ref[...])
    for index in range(MOMS * TIMES):
        for copy in copies(index):
            copy.wait()


def last(row, pairing, got, tables, high, low, sums, out):
    slab = high.shape[1]
    return call(
        last_body,
        [
            ((2, MOMS, TIMES, slab, N, N), BF16, ANY),
            ((64, 128), F32, VMEM),
        ],
        [pltpu.VMEM((4, 2, N, N), BF16), pltpu.SemaphoreType.DMA((4, 2))],
        16,
        3 * 2 * 2 * 512 * 512 * 256 * 4,
        10 << 20,
        [SMEM, SMEM] + [VMEM] * 8 + [ANY],
        {10: 0},
    )(row, pairing, got, *tables, high, low, sums, out)


def empty_body(out_ref):
    del out_ref


def shards(elementals, perambulators, owners, pairing):
    slab = elementals.shape[2]
    quarter = lax.axis_index("mom").astype(jnp.int32)

    mine = perambulators[0].reshape(TIMES, 2, 64, 4, N)
    mine = lax.dynamic_index_in_dim(mine, quarter, 3, keepdims=False)
    mine = mine.reshape(4, 64, N).transpose(1, 0, 2)
    pieces = lax.all_to_all(mine, "modes", 0, 0, tiled=True)
    piece = jnp.concatenate(
        [
            lax.dynamic_slice(pieces, (owners[time], 2 * time, 0), (1, 2, N))
            for time in range(TIMES)
        ],
        axis=1,
    )
    own = lax.all_to_all(jnp.broadcast_to(piece, (64, 4, N)), "modes", 0, 0, tiled=True)
    own = own.transpose(1, 0, 2)
    quarters = [own] + [
        lax.ppermute(own, "mom", [((i + shift) % 4, i) for i in range(4)]) for shift in (1, 2, 3)
    ]

    high, low = turn(elementals)
    tables = weights(quarter[None], quarters)
    out = pl.pallas_call(
        empty_body,
        out_shape=jax.ShapeDtypeStruct((2, MOMS, TIMES, slab, N, N), BF16),
        out_specs=ANY,
    )()
    sums = jnp.zeros((64, 128), F32)
    for shift in range(4):
        sent = first(quarters[shift], high, low)
        got = lax.all_to_all(sent, "modes", 0, 0, tiled=True)
        row = (quarter + shift) % 4
        out, sums = last(row[None], pairing, got, tables, high, low, sums, out)
    sums = lax.all_to_all(sums, "modes", 0, 0, tiled=True)
    correlator = jnp.sum(sums[:, :8], axis=0).reshape(2, MOMS, TIMES) * float(N) ** -1.5
    return out, correlator


def solution(mesh):
    placed = (
        P(None, "mom", "modes", None, None),
        P("modes", None, None, None, None),
        P(),
        P("mom"),
    )
    return jax.shard_map(
        shards,
        mesh=mesh,
        in_specs=placed,
        out_specs=(P(None, "mom", None, "modes", None, None), P(None, "mom", None)),
        check_vma=False,
    )
```

```python
import functools

import jax
import jax.numpy as jnp
from jax import lax
from jax.experimental import pallas as pl
from jax.experimental.pallas import tpu as pltpu
from jax.sharding import PartitionSpec as P

N = 256
ROWS = 64
MOMS = 2
TIMES = 2
F32 = jnp.float32
BF16 = jnp.bfloat16
VMEM = pl.BlockSpec(memory_space=pltpu.VMEM)
SMEM = pl.BlockSpec(memory_space=pltpu.SMEM)
ANY = pl.BlockSpec(memory_space=pl.ANY)


def halves(x):
    high = x.astype(BF16)
    return high, (x - high.astype(F32)).astype(BF16)


def dot(a, b):
    return jnp.dot(a, b, preferred_element_type=F32)


def dot3(a, b):
    left = jnp.concatenate([a[0], a[0], a[1]], axis=1)
    return dot(left, jnp.concatenate([b[0], b[1], b[0]], axis=0))


def params(flops, nbytes):
    return dict(
        cost_estimate=pl.CostEstimate(flops=flops, bytes_accessed=nbytes, transcendentals=0),
    )


def turn_body(elem_ref, high_ref, low_ref):
    for comp in range(2):
        high, low = halves(elem_ref[comp, 0, 0].T)
        high_ref[0, 0, comp * N : (comp + 1) * N, :] = high
        low_ref[0, 0, comp * N : (comp + 1) * N, :] = low


def turn(elementals):
    slab = elementals.shape[2]
    out = jax.ShapeDtypeStruct((MOMS, slab, 2 * N, N), BF16)
    spec = pl.BlockSpec((1, 1, 2 * N, N), lambda m, a: (m, a, 0, 0))
    return pl.pallas_call(
        turn_body,
        grid=(MOMS, slab),
        out_shape=[out, out],
        in_specs=[pl.BlockSpec((2, 1, 1, N, N), lambda m, a: (0, m, a, 0, 0))],
        out_specs=[spec, spec],
        **params(1 << 20, 8 << 20),
    )(elementals)


def first_body(count, *refs):
    perams, (high_hbm, low_hbm, send_hbm), refs = refs[:count], refs[count : count + 3], refs[count + 3 :]
    wh_ref, wl_ref, high_ref, low_ref, send_ref, in_sems, out_sems = refs
    slab = high_ref.shape[1]

    def loads(mom, a):
        return [
            pltpu.make_async_copy(src.at[mom, a], dst.at[mom, a], in_sems.at[which, mom, a])
            for which, (src, dst) in enumerate(((high_hbm, high_ref), (low_hbm, low_ref)))
        ]

    def store(mom):
        rows = pl.ds(mom * count * 32, count * 32)
        return pltpu.make_async_copy(send_ref.at[mom], send_hbm.at[:, rows, :], out_sems.at[mom])

    for mom in range(MOMS):
        for a in range(slab):
            for copy in loads(mom, a):
                copy.start()
    for index, ref in enumerate(perams):
        for time in range(TIMES):
            re = ref[2 * time]
            im = ref[2 * time + 1]
            for comp, left, right in ((0, re, -im), (1, im, re)):
                row = ((index * TIMES + time) * 2 + comp) * ROWS
                for col, part in ((0, left), (N, right)):
                    high, low = halves(part)
                    wh_ref[row : row + ROWS, col : col + N] = high
                    wl_ref[row : row + ROWS, col : col + N] = low

    for mom in range(MOMS):
        flat = send_ref.at[mom].reshape(64 * count * 32, 128)

        def step(a, carry, mom=mom, flat=flat):
            for copy in loads(mom, a):
                copy.wait()
            elem = (high_ref[mom, a], low_ref[mom, a])
            for index in range(count):
                rows = slice(index * 4 * ROWS, (index + 1) * 4 * ROWS)
                product = dot3((wh_ref[rows], wl_ref[rows]), elem)
                for time in range(TIMES):
                    for comp in range(2):
                        row = (2 * time + comp) * ROWS
                        for half in range(2):
                            start = ((index * TIMES + time) * 2 + half) * 8 + comp * 4 + a
                            flat[pl.ds(start, ROWS, stride=count * 32), :] = product[
                                row : row + ROWS, half * 128 : (half + 1) * 128
                            ]
            return carry

        lax.fori_loop(0, slab, step, 0)
        store(mom).start()
    for mom in range(MOMS):
        store(mom).wait()


def first(perams, high, low):
    count, slab = len(perams), high.shape[1]
    return pl.pallas_call(
        functools.partial(first_body, count),
        in_specs=[VMEM] * count + [ANY, ANY],
        out_specs=ANY,
        out_shape=jax.ShapeDtypeStruct((64, MOMS * count * 32, 128), F32),
        scratch_shapes=[pltpu.VMEM((count * 4 * ROWS, 2 * N), BF16)] * 2
        + [pltpu.VMEM((MOMS, slab, 2 * N, N), BF16)] * 2
        + [
            pltpu.VMEM((MOMS, 64, count * 32, 128), F32),
            pltpu.SemaphoreType.DMA((2, MOMS, slab)),
            pltpu.SemaphoreType.DMA((MOMS,)),
        ],
        **params(count * 3 * 2 * 256 * 512 * 256 * 8, 6 << 20),
    )(*perams, high, low)


def weights_body(quarter_ref, own_ref, g1_ref, g2_ref, g3_ref, vh_ref, vl_ref, wh_ref, wl_ref):
    quarter = quarter_ref[0]
    nat = lax.broadcasted_iota(jnp.int32, (N, N), 0)
    col = lax.broadcasted_iota(jnp.int32, (N, N), 1)
    place = 4 * (col & 63) + (quarter ^ (col >> 6))
    order = (nat == place).astype(F32).astype(BF16)
    row = lax.broadcasted_iota(jnp.int32, (2 * N, 2 * N), 0)
    col = lax.broadcasted_iota(jnp.int32, (2 * N, 2 * N), 1)
    place = N * ((col >> 2) & 1) + 4 * (col >> 3) + (col & 3)
    spread = (row == place).astype(F32).astype(BF16)
    for time in range(TIMES):
        parts = []
        for comp in range(2):
            index = 2 * time + comp
            stacked = jnp.concatenate(
                [ref[index] for ref in (own_ref, g1_ref, g2_ref, g3_ref)], axis=0
            )
            parts.append([dot(order, part) for part in halves(stacked)])
        for which, v_ref, w_ref in ((0, vh_ref, wh_ref), (1, vl_ref, wl_ref)):
            re = parts[0][which]
            im = parts[1][which]
            re_t = re.T.astype(BF16)
            im_t = im.T
            v_ref[time, :N, :N] = re_t
            v_ref[time, :N, N:] = im_t.astype(BF16)
            v_ref[time, N:, :N] = (-im_t).astype(BF16)
            v_ref[time, N:, N:] = re_t
            re = re.astype(BF16)
            minus = (-im).astype(BF16)
            im = im.astype(BF16)
            w_ref[time, :N] = (dot(re, spread[:N]) + dot(minus, spread[N:])).astype(BF16)
            w_ref[time, N:] = (dot(im, spread[:N]) + dot(re, spread[N:])).astype(BF16)


def weights(quarter, pieces):
    return pl.pallas_call(
        weights_body,
        in_specs=[SMEM] + [VMEM] * 4,
        out_specs=[VMEM] * 4,
        out_shape=[jax.ShapeDtypeStruct((TIMES, 2 * N, 2 * N), BF16)] * 4,
        **params(2 * 2 * 2 * 2 * 256 * 512 * 512, 5 << 20),
    )(quarter, *pieces)


def add_sums(sums_ref, total_ref, index, start, real, imag):
    @pl.when(start)
    def _():
        total_ref[...] = sums_ref[...]

    lane = lax.broadcasted_iota(jnp.int32, (64, 128), 1)
    total_ref[...] += jnp.where(lane == index, real, 0.0) + jnp.where(lane == index + 4, imag, 0.0)


def last_body(row_ref, pair_ref, got_ref, vh_ref, vl_ref, wh_ref, wl_ref, *refs):
    del row_ref, pair_ref
    out_ref = refs[-1] if len(refs) == 2 else refs[-2]
    got = jnp.concatenate(
        [got_ref[:, half * 8 : (half + 1) * 8, :].reshape(512, 128) for half in range(2)], axis=1
    )
    second = dot3((wh_ref[0], wl_ref[0]), halves(got))
    high, low = [jnp.concatenate([part[:N], part[N:]], axis=1) for part in halves(second)]
    full = dot3((high, low), (vh_ref[0], vl_ref[0]))
    re, im = full[:, :N], full[:, N:]
    out_ref[0, 0, 0, 0] = re.astype(BF16)
    out_ref[1, 0, 0, 0] = im.astype(BF16)
    if len(refs) == 2:
        return
    high_ref, low_ref, sums_ref, _, _, total_ref = refs
    sink = high_ref[0, 0].astype(F32) + low_ref[0, 0].astype(F32)
    sink_re, sink_im = sink[:N], sink[N:]
    real = jnp.sum(sink_re * re + sink_im * im)
    imag = jnp.sum(sink_re * im - sink_im * re)
    time, mom = pl.program_id(0), pl.program_id(1)
    add_sums(sums_ref, total_ref, mom * TIMES + time, (time == 0) & (mom == 0), real, imag)


TABLE = pl.BlockSpec((1, 2 * N, 2 * N), lambda t, m, row, pair: (t, 0, 0))
ELEM = pl.BlockSpec((1, 1, 2 * N, N), lambda t, m, row, pair: (pair[m], row[0], 0, 0))


def last(row, pairing, got, count, which, tables, high, low, sums, out):
    whole = pl.BlockSpec((64, 128), lambda t, m, row, pair: (0, 0))
    block = pl.BlockSpec(
        (64, 16, 128), lambda t, m, row, pair: (0, (m * count + which) * TIMES + t, 0)
    )
    with_sums = sums is not None
    result = pl.pallas_call(
        last_body,
        grid_spec=pltpu.PrefetchScalarGridSpec(
            num_scalar_prefetch=2,
            grid=(TIMES, MOMS),
            in_specs=[block] + [TABLE] * 4 + ([ELEM, ELEM, whole] if with_sums else []) + [ANY],
            out_specs=[
                pl.BlockSpec((2, 1, 1, 1, N, N), lambda t, m, row, pair: (0, m, t, row[0], 0, 0))
            ]
            + ([whole] if with_sums else []),
        ),
        out_shape=[jax.ShapeDtypeStruct(out.shape, BF16)]
        + ([jax.ShapeDtypeStruct((64, 128), F32)] if with_sums else []),
        input_output_aliases={10 if with_sums else 7: 0},
        **params(3 * 2 * 2 * 512 * 512 * 256 * 4, 10 << 20),
    )(row, pairing, got, *tables, *((high, low, sums) if with_sums else ()), out)
    return result if with_sums else (result[0], None)


def dual_body(row_ref, pair_ref, vh_ref, vl_ref, wh_ref, wl_ref, high_ref, low_ref, out_ref):
    del row_ref, pair_ref
    high, low = [
        jnp.concatenate([ref[0, 0, :N], ref[0, 0, N:]], axis=1) for ref in (high_ref, low_ref)
    ]
    second = lax.dot_general(
        jnp.concatenate([high, high, low], axis=1),
        jnp.concatenate([vh_ref[0], vl_ref[0], vh_ref[0]], axis=1),
        (((1,), (1,)), ((), ())),
        preferred_element_type=F32,
    )
    high, low = halves(jnp.concatenate([second[:, :N], second[:, N:]], axis=0))
    full = lax.dot_general(
        jnp.concatenate([wh_ref[0], wh_ref[0], wl_ref[0]], axis=0),
        jnp.concatenate([high, low, high], axis=0),
        (((0,), (0,)), ((), ())),
        preferred_element_type=F32,
    )
    for half in range(2):
        out_ref[:, half * 8 : (half + 1) * 8, :] = full[:, half * 128 : (half + 1) * 128].reshape(
            64, 8, 128
        )


def dual(row, pairing, tables, high, low):
    return pl.pallas_call(
        dual_body,
        grid_spec=pltpu.PrefetchScalarGridSpec(
            num_scalar_prefetch=2,
            grid=(TIMES, MOMS),
            in_specs=[TABLE] * 4 + [ELEM, ELEM],
            out_specs=pl.BlockSpec((64, 16, 128), lambda t, m, row, pair: (0, m * TIMES + t, 0)),
        ),
        out_shape=jax.ShapeDtypeStruct((64, 64, 128), F32),
        **params(3 * 2 * 2 * 512 * 512 * 256 * 4, 8 << 20),
    )(row, pairing, *tables, high, low)


def meet_body(got_ref, dual_hbm, sums_hbm, total_ref, dual_ref, sums_ref, sems):
    copies = [
        pltpu.make_async_copy(
            dual_hbm.at[:, index * 16 : (index + 1) * 16, :], dual_ref.at[index], sems.at[index]
        )
        for index in range(MOMS * TIMES)
    ]
    copies.append(pltpu.make_async_copy(sums_hbm, sums_ref, sems.at[MOMS * TIMES]))
    for copy in copies:
        copy.start()
    lane = lax.broadcasted_iota(jnp.int32, (64, 128), 1)
    upper = (lax.broadcasted_iota(jnp.int32, (1024, 128), 0) & 4) == 0
    total = jnp.zeros((64, 128), F32)
    for index in range(MOMS * TIMES):
        copies[index].wait()
        got = got_ref[:, index * 16 : (index + 1) * 16, :].reshape(1024, 128)
        other = dual_ref[index].reshape(1024, 128)
        real = jnp.sum(got * other)
        turned = jnp.where(upper, -pltpu.roll(other, 1020, 0), pltpu.roll(other, 4, 0))
        imag = jnp.sum(got * turned)
        total += jnp.where(lane == index, real, 0.0) + jnp.where(lane == index + 4, imag, 0.0)
    copies[-1].wait()
    total_ref[...] = total + sums_ref[...]


def meet(got, other, sums):
    hbm = pl.BlockSpec(memory_space=pltpu.HBM)
    return pl.pallas_call(
        meet_body,
        in_specs=[VMEM, hbm, hbm],
        out_specs=VMEM,
        out_shape=jax.ShapeDtypeStruct((64, 128), F32),
        scratch_shapes=[
            pltpu.VMEM((MOMS * TIMES, 64, 16, 128), F32),
            pltpu.VMEM((64, 128), F32),
            pltpu.SemaphoreType.DMA((MOMS * TIMES + 1,)),
        ],
        compiler_params=pltpu.CompilerParams(vmem_limit_bytes=8 << 20),
        **params(1 << 21, 4 << 20),
    )(got, other, sums)


def empty_body(out_ref):
    del out_ref


def shards(elementals, perambulators, owners, pairing):
    slab = elementals.shape[2]
    quarter = lax.axis_index("mom").astype(jnp.int32)

    mine = perambulators[0].reshape(TIMES, 2, 64, 4, N)
    mine = lax.dynamic_index_in_dim(mine, quarter, 3, keepdims=False)
    mine = mine.reshape(4, 64, N).transpose(1, 0, 2)
    pieces = lax.all_to_all(mine, "modes", 0, 0, tiled=True)
    piece = jnp.concatenate(
        [
            lax.dynamic_slice(pieces, (owners[time], 2 * time, 0), (1, 2, N))
            for time in range(TIMES)
        ],
        axis=1,
    )
    own = lax.all_to_all(jnp.broadcast_to(piece, (64, 4, N)), "modes", 0, 0, tiled=True)
    own = own.transpose(1, 0, 2)
    by_core = lax.ppermute(own, "mom", [(i ^ 1, i) for i in range(4)])
    by_chip = lax.ppermute(own, "mom", [(i ^ 2, i) for i in range(4)])
    by_both = lax.ppermute(by_chip, "mom", [(i ^ 1, i) for i in range(4)])
    quarters = [own, by_core, by_chip, by_both]

    high, low = turn(elementals)
    tables = weights(quarter[None], quarters)
    out = pl.pallas_call(
        empty_body,
        out_shape=jax.ShapeDtypeStruct((2, MOMS, TIMES, slab, N, N), BF16),
        out_specs=ANY,
    )()
    sums = jnp.zeros((64, 128), F32)
    other = dual((quarter ^ 3)[None], pairing, tables, high, low)
    for name, group in enumerate(((0,), (1, 2), (3,))):
        sent = first([quarters[shift] for shift in group], high, low)
        got = lax.all_to_all(sent, "modes", 0, 0, tiled=True)
        if name < 2:
            for which, shift in enumerate(group):
                row = (quarter ^ shift)[None]
                out, sums = last(row, pairing, got, len(group), which, tables, high, low, sums, out)
    sums = meet(got, other, sums)
    sums = lax.all_to_all(sums, "modes", 0, 0, tiled=True)
    out, _ = last((quarter ^ 3)[None], pairing, got, 1, 0, tables, high, low, None, out)
    correlator = jnp.sum(sums[:, :8], axis=0).reshape(2, MOMS, TIMES) * float(N) ** -1.5
    return out, correlator


def solution(mesh):
    placed = (
        P(None, "mom", "modes", None, None),
        P("modes", None, None, None, None),
        P(),
        P("mom"),
    )
    return jax.shard_map(
        shards,
        mesh=mesh,
        in_specs=placed,
        out_specs=(P(None, "mom", None, "modes", None, None), P(None, "mom", None)),
        check_vma=False,
    )
```

```python
import functools

import jax
import jax.numpy as jnp
from jax import lax
from jax.experimental import pallas as pl
from jax.experimental.pallas import tpu as pltpu
from jax.sharding import PartitionSpec as P

N = 256
ROWS = 64
MOMS = 2
TIMES = 2
F32 = jnp.float32
BF16 = jnp.bfloat16
VMEM = pl.BlockSpec(memory_space=pltpu.VMEM)
SMEM = pl.BlockSpec(memory_space=pltpu.SMEM)
ANY = pl.BlockSpec(memory_space=pl.ANY)


def halves(x):
    high = x.astype(BF16)
    return high, (x - high.astype(F32)).astype(BF16)


def dot(a, b):
    return jnp.dot(a, b, preferred_element_type=F32)


def dot3(a, b):
    left = jnp.concatenate([a[0], a[0], a[1]], axis=1)
    right = jnp.concatenate([b[0], b[1], b[0]], axis=0)
    if right.shape[1] > N:
        parts = [dot(left, right[:, col : col + N]) for col in range(0, right.shape[1], N)]
        return jnp.concatenate(parts, axis=1)
    half = left.shape[0] // 2
    return jnp.concatenate([dot(left[:half], right), dot(left[half:], right)], axis=0)


def params(flops, nbytes):
    return dict(
        cost_estimate=pl.CostEstimate(flops=flops, bytes_accessed=nbytes, transcendentals=0),
    )


def turn_body(elem_ref, high_ref, low_ref):
    for comp in range(2):
        high, low = halves(elem_ref[comp, 0, 0].T)
        high_ref[0, 0, comp * N : (comp + 1) * N, :] = high
        low_ref[0, 0, comp * N : (comp + 1) * N, :] = low


def turn(elementals):
    slab = elementals.shape[2]
    out = jax.ShapeDtypeStruct((MOMS, slab, 2 * N, N), BF16)
    spec = pl.BlockSpec((1, 1, 2 * N, N), lambda m, a: (m, a, 0, 0))
    return pl.pallas_call(
        turn_body,
        grid=(MOMS, slab),
        out_shape=[out, out],
        in_specs=[pl.BlockSpec((2, 1, 1, N, N), lambda m, a: (0, m, a, 0, 0))],
        out_specs=[spec, spec],
        **params(1 << 20, 8 << 20),
    )(elementals)


def first_body(count, *refs):
    perams, (high_hbm, low_hbm, send_hbm), refs = refs[:count], refs[count : count + 3], refs[count + 3 :]
    wh_ref, wl_ref, high_ref, low_ref, send_ref, in_sems, out_sems = refs
    slab = high_ref.shape[1]

    def loads(mom, a):
        return [
            pltpu.make_async_copy(src.at[mom, a], dst.at[mom, a], in_sems.at[which, mom, a])
            for which, (src, dst) in enumerate(((high_hbm, high_ref), (low_hbm, low_ref)))
        ]

    def store(mom, index):
        rows = pl.ds((mom * count + index) * 32, 32)
        return pltpu.make_async_copy(
            send_ref.at[mom, index], send_hbm.at[:, rows, :], out_sems.at[mom, index]
        )

    for mom in range(MOMS):
        for a in range(slab):
            for copy in loads(mom, a):
                copy.start()
    for index, ref in enumerate(perams):
        for time in range(TIMES):
            re = ref[2 * time]
            im = ref[2 * time + 1]
            for comp, left, right in ((0, re, -im), (1, im, re)):
                row = ((index * TIMES + time) * 2 + comp) * ROWS
                for col, part in ((0, left), (N, right)):
                    high, low = halves(part)
                    wh_ref[row : row + ROWS, col : col + N] = high
                    wl_ref[row : row + ROWS, col : col + N] = low

    for mom in range(MOMS):
        for index in range(count):
            flat = send_ref.at[mom, index].reshape(64 * 32, 128)
            rows = slice(index * 4 * ROWS, (index + 1) * 4 * ROWS)

            def step(a, carry, mom=mom, index=index, flat=flat, rows=rows):
                if index == 0:
                    for copy in loads(mom, a):
                        copy.wait()
                product = dot3((wh_ref[rows], wl_ref[rows]), (high_ref[mom, a], low_ref[mom, a]))
                for time in range(TIMES):
                    for comp in range(2):
                        row = (2 * time + comp) * ROWS
                        for half in range(2):
                            start = (time * 2 + half) * 8 + comp * 4 + a
                            flat[pl.ds(start, ROWS, stride=32), :] = product[
                                row : row + ROWS, half * 128 : (half + 1) * 128
                            ]
                return carry

            lax.fori_loop(0, slab, step, 0)
            store(mom, index).start()
    for mom in range(MOMS):
        for index in range(count):
            store(mom, index).wait()


def first(perams, high, low):
    count, slab = len(perams), high.shape[1]
    return pl.pallas_call(
        functools.partial(first_body, count),
        in_specs=[VMEM] * count + [ANY, ANY],
        out_specs=ANY,
        out_shape=jax.ShapeDtypeStruct((64, MOMS * count * 32, 128), F32),
        scratch_shapes=[pltpu.VMEM((count * 4 * ROWS, 2 * N), BF16)] * 2
        + [pltpu.VMEM((MOMS, slab, 2 * N, N), BF16)] * 2
        + [
            pltpu.VMEM((MOMS, count, 64, 32, 128), F32),
            pltpu.SemaphoreType.DMA((2, MOMS, slab)),
            pltpu.SemaphoreType.DMA((MOMS, count)),
        ],
        **params(count * 3 * 2 * 256 * 512 * 256 * 8, 6 << 20),
    )(*perams, high, low)


def weights_body(quarter_ref, own_ref, g1_ref, g2_ref, g3_ref, vh_ref, vl_ref, wh_ref, wl_ref):
    quarter = quarter_ref[0]
    nat = lax.broadcasted_iota(jnp.int32, (N, N), 0)
    col = lax.broadcasted_iota(jnp.int32, (N, N), 1)
    place = 4 * (col & 63) + (quarter ^ (col >> 6))
    order = (nat == place).astype(F32).astype(BF16)
    row = lax.broadcasted_iota(jnp.int32, (2 * N, 2 * N), 0)
    col = lax.broadcasted_iota(jnp.int32, (2 * N, 2 * N), 1)
    place = N * ((col >> 2) & 1) + 4 * (col >> 3) + (col & 3)
    spread = (row == place).astype(F32).astype(BF16)
    for time in range(TIMES):
        parts = []
        for comp in range(2):
            index = 2 * time + comp
            stacked = jnp.concatenate(
                [ref[index] for ref in (own_ref, g1_ref, g2_ref, g3_ref)], axis=0
            )
            parts.append([dot(order, part) for part in halves(stacked)])
        for which, v_ref, w_ref in ((0, vh_ref, wh_ref), (1, vl_ref, wl_ref)):
            re = parts[0][which]
            im = parts[1][which]
            re_t = re.T.astype(BF16)
            im_t = im.T
            v_ref[time, :N, :N] = re_t
            v_ref[time, :N, N:] = im_t.astype(BF16)
            v_ref[time, N:, :N] = (-im_t).astype(BF16)
            v_ref[time, N:, N:] = re_t
            re = re.astype(BF16)
            minus = (-im).astype(BF16)
            im = im.astype(BF16)
            w_ref[time, :N] = (dot(re, spread[:N]) + dot(minus, spread[N:])).astype(BF16)
            w_ref[time, N:] = (dot(im, spread[:N]) + dot(re, spread[N:])).astype(BF16)


def weights(quarter, pieces):
    return pl.pallas_call(
        weights_body,
        in_specs=[SMEM] + [VMEM] * 4,
        out_specs=[VMEM] * 4,
        out_shape=[jax.ShapeDtypeStruct((TIMES, 2 * N, 2 * N), BF16)] * 4,
        **params(2 * 2 * 2 * 2 * 256 * 512 * 512, 5 << 20),
    )(quarter, *pieces)


def add_sums(sums_ref, total_ref, index, start, real, imag):
    @pl.when(start)
    def _():
        total_ref[...] = sums_ref[...]

    lane = lax.broadcasted_iota(jnp.int32, (64, 128), 1)
    total_ref[...] += jnp.where(lane == index, real, 0.0) + jnp.where(lane == index + 4, imag, 0.0)


def last_body(row_ref, pair_ref, got_ref, vh_ref, vl_ref, wh_ref, wl_ref, *refs):
    del row_ref, pair_ref
    out_ref = refs[-1] if len(refs) == 2 else refs[-2]
    got = jnp.concatenate(
        [got_ref[:, half * 8 : (half + 1) * 8, :].reshape(512, 128) for half in range(2)], axis=1
    )
    second = dot3((wh_ref[0], wl_ref[0]), halves(got))
    high, low = [jnp.concatenate([part[:N], part[N:]], axis=1) for part in halves(second)]
    full = dot3((high, low), (vh_ref[0], vl_ref[0]))
    re, im = full[:, :N], full[:, N:]
    out_ref[0, 0, 0, 0] = re.astype(BF16)
    out_ref[1, 0, 0, 0] = im.astype(BF16)
    if len(refs) == 2:
        return
    high_ref, low_ref, sums_ref, _, _, total_ref = refs
    sink = high_ref[0, 0].astype(F32) + low_ref[0, 0].astype(F32)
    sink_re, sink_im = sink[:N], sink[N:]
    real = jnp.sum(sink_re * re + sink_im * im)
    imag = jnp.sum(sink_re * im - sink_im * re)
    time, which, mom = pl.program_id(0), pl.program_id(1), pl.program_id(2)
    start = (time == 0) & (which == 0) & (mom == 0)
    add_sums(sums_ref, total_ref, mom * TIMES + time, start, real, imag)


def specs(count):
    table = pl.BlockSpec((1, 2 * N, 2 * N), lambda t, w, m, rows, pair: (t, 0, 0))
    elem = pl.BlockSpec((1, 1, 2 * N, N), lambda t, w, m, rows, pair: (pair[m], rows[w], 0, 0))
    block = pl.BlockSpec(
        (64, 16, 128), lambda t, w, m, rows, pair: (0, (m * count + w) * TIMES + t, 0)
    )
    return [table] * 4, [elem] * 2, block


def last(rows, pairing, got, tables, high, low, sums, out):
    count = rows.shape[0]
    table, elem, block = specs(count)
    whole = pl.BlockSpec((64, 128), lambda t, w, m, rows, pair: (0, 0))
    with_sums = sums is not None
    result = pl.pallas_call(
        last_body,
        grid_spec=pltpu.PrefetchScalarGridSpec(
            num_scalar_prefetch=2,
            grid=(TIMES, count, MOMS),
            in_specs=[block] + table + (elem + [whole] if with_sums else []) + [ANY],
            out_specs=[
                pl.BlockSpec(
                    (2, 1, 1, 1, N, N), lambda t, w, m, rows, pair: (0, m, t, rows[w], 0, 0)
                )
            ]
            + ([whole] if with_sums else []),
        ),
        out_shape=[jax.ShapeDtypeStruct(out.shape, BF16)]
        + ([jax.ShapeDtypeStruct((64, 128), F32)] if with_sums else []),
        input_output_aliases={10 if with_sums else 7: 0},
        **params(count * 3 * 2 * 2 * 512 * 512 * 256 * 4, count * (10 << 20)),
    )(rows, pairing, got, *tables, *((high, low, sums) if with_sums else ()), out)
    return result if with_sums else (result[0], None)


def dual_body(rows_ref, pair_ref, vh_ref, vl_ref, wh_ref, wl_ref, high_ref, low_ref, out_ref):
    del rows_ref, pair_ref
    high, low = [
        jnp.concatenate([ref[0, 0, :N], ref[0, 0, N:]], axis=1) for ref in (high_ref, low_ref)
    ]
    left = jnp.concatenate([high, high, low], axis=1)
    second = []
    for comp in range(2):
        rows = slice(comp * N, (comp + 1) * N)
        right = jnp.concatenate([vh_ref[0, rows], vl_ref[0, rows], vh_ref[0, rows]], axis=1)
        second.append(
            lax.dot_general(left, right, (((1,), (1,)), ((), ())), preferred_element_type=F32)
        )
    high, low = halves(jnp.concatenate(second, axis=0))
    right = jnp.concatenate([high, low, high], axis=0)
    for part in range(2):
        cols = slice(part * N, (part + 1) * N)
        left = jnp.concatenate([wh_ref[0, :, cols], wh_ref[0, :, cols], wl_ref[0, :, cols]], axis=0)
        full = lax.dot_general(left, right, (((0,), (0,)), ((), ())), preferred_element_type=F32)
        for half in range(2):
            out_ref[part * 32 : (part + 1) * 32, half * 8 : (half + 1) * 8, :] = full[
                :, half * 128 : (half + 1) * 128
            ].reshape(32, 8, 128)


def dual(rows, pairing, tables, high, low):
    count = rows.shape[0]
    table, elem, block = specs(count)
    return pl.pallas_call(
        dual_body,
        grid_spec=pltpu.PrefetchScalarGridSpec(
            num_scalar_prefetch=2,
            grid=(TIMES, count, MOMS),
            in_specs=table + elem,
            out_specs=block,
        ),
        out_shape=jax.ShapeDtypeStruct((64, MOMS * count * TIMES * 16, 128), F32),
        **params(count * 3 * 2 * 2 * 512 * 512 * 256 * 4, count * (8 << 20)),
    )(rows, pairing, *tables, high, low)


def meet_body(got_hbm, dual_hbm, sums_ref, total_ref, got_ref, dual_ref, sems):
    steps, share = sems.shape[1], got_ref.shape[0] // sems.shape[1]
    blocks = got_ref.shape[1] // 16
    copies = []
    for step in range(steps):
        part = pl.ds(step * share, share)
        copies.append(
            [
                pltpu.make_async_copy(src.at[part], dst.at[part], sems.at[which, step])
                for which, (src, dst) in enumerate(((got_hbm, got_ref), (dual_hbm, dual_ref)))
            ]
        )
        for copy in copies[-1]:
            copy.start()
    sums = [[jnp.zeros((8, 128), F32)] * (MOMS * TIMES) for _ in range(2)]
    for step in range(steps):
        for copy in copies[step]:
            copy.wait()
        part = slice(step * share, (step + 1) * share)
        for block in range(blocks):
            index = block // (blocks // MOMS) * TIMES + block % TIMES
            for half in range(2):
                rows = slice(block * 16 + half * 8, block * 16 + half * 8 + 8)
                got = got_ref[part, rows, :]
                other = dual_ref[part, rows, :]
                sums[0][index] += jnp.sum(got * other, axis=0)
                sums[1][index] += jnp.sum(got * pltpu.roll(other, 4, 1), axis=0)
    sign = jnp.where((lax.broadcasted_iota(jnp.int32, (8, 128), 0) & 4) == 0, -1.0, 1.0)
    lane = lax.broadcasted_iota(jnp.int32, (64, 128), 1)
    total = sums_ref[...]
    for index in range(MOMS * TIMES):
        total += jnp.where(lane == index, jnp.sum(sums[0][index]), 0.0)
        total += jnp.where(lane == index + 4, jnp.sum(sign * sums[1][index]), 0.0)
    total_ref[...] = total


def meet(got, other, sums):
    return pl.pallas_call(
        meet_body,
        in_specs=[ANY, ANY, VMEM],
        out_specs=VMEM,
        out_shape=jax.ShapeDtypeStruct((64, 128), F32),
        scratch_shapes=[pltpu.VMEM(got.shape, F32)] * 2 + [pltpu.SemaphoreType.DMA((2, 8))],
        **params(1 << 22, 8 << 20),
    )(got, other, sums)


def empty_body(out_ref):
    del out_ref


def shards(elementals, perambulators, owners, pairing):
    slab = elementals.shape[2]
    quarter = lax.axis_index("mom").astype(jnp.int32)

    mine = perambulators[0].reshape(TIMES, 2, 64, 4, N)
    mine = lax.dynamic_index_in_dim(mine, quarter, 3, keepdims=False)
    mine = mine.reshape(4, 64, N).transpose(1, 0, 2)
    pieces = lax.all_to_all(mine, "modes", 0, 0, tiled=True)
    piece = jnp.concatenate(
        [
            lax.dynamic_slice(pieces, (owners[time], 2 * time, 0), (1, 2, N))
            for time in range(TIMES)
        ],
        axis=1,
    )
    own = lax.all_to_all(jnp.broadcast_to(piece, (64, 4, N)), "modes", 0, 0, tiled=True)
    own = own.transpose(1, 0, 2)
    by_core = lax.ppermute(own, "mom", [(i ^ 1, i) for i in range(4)])
    by_chip = lax.ppermute(own, "mom", [(i ^ 2, i) for i in range(4)])
    by_both = lax.ppermute(by_chip, "mom", [(i ^ 1, i) for i in range(4)])
    quarters = [own, by_core, by_chip, by_both]

    high, low = turn(elementals)
    tables = weights(quarter[None], quarters)
    out = pl.pallas_call(
        empty_body,
        out_shape=jax.ShapeDtypeStruct((2, MOMS, TIMES, slab, N, N), BF16),
        out_specs=ANY,
    )()
    sums = jnp.zeros((64, 128), F32)
    rows = jnp.stack([quarter ^ 2, quarter ^ 3])
    other = dual(rows, pairing, tables, high, low)
    gots = []
    for name in range(2):
        sent = first(quarters[2 * name : 2 * name + 2], high, low)
        gots.append(lax.all_to_all(sent, "modes", 0, 0, tiled=True))
    near = jnp.stack([quarter, quarter ^ 1])
    out, sums = last(near, pairing, gots[0], tables, high, low, sums, out)
    sums = meet(gots[1], other, sums)
    sums = lax.all_to_all(sums, "modes", 0, 0, tiled=True)
    out, _ = last(rows, pairing, gots[1], tables, high, low, None, out)
    correlator = jnp.sum(sums[:, :8], axis=0).reshape(2, MOMS, TIMES) * float(N) ** -1.5
    return out, correlator


def solution(mesh):
    placed = (
        P(None, "mom", "modes", None, None),
        P("modes", None, None, None, None),
        P(),
        P("mom"),
    )
    return jax.shard_map(
        shards,
        mesh=mesh,
        in_specs=placed,
        out_specs=(P(None, "mom", None, "modes", None, None), P(None, "mom", None)),
        check_vma=False,
    )
```

```python
import functools

import jax
import jax.numpy as jnp
from jax import lax
from jax.experimental import pallas as pl
from jax.experimental.pallas import tpu as pltpu
from jax.sharding import PartitionSpec as P

N = 256
ROWS = 64
MOMS = 2
TIMES = 2
F32 = jnp.float32
BF16 = jnp.bfloat16
VMEM = pl.BlockSpec(memory_space=pltpu.VMEM)
SMEM = pl.BlockSpec(memory_space=pltpu.SMEM)
ANY = pl.BlockSpec(memory_space=pl.ANY)


def halves(x):
    high = x.astype(BF16)
    return high, (x - high.astype(F32)).astype(BF16)


def dot(a, b):
    return jnp.dot(a, b, preferred_element_type=F32)


def params(flops, nbytes):
    return dict(
        cost_estimate=pl.CostEstimate(flops=flops, bytes_accessed=nbytes, transcendentals=0),
    )


def turn_body(elem_ref, high_ref, low_ref):
    for comp in range(2):
        high, low = halves(elem_ref[comp, 0, 0].T)
        high_ref[0, 0, comp * N : (comp + 1) * N, :] = high
        low_ref[0, 0, comp * N : (comp + 1) * N, :] = low


def turn(elementals):
    slab = elementals.shape[2]
    out = jax.ShapeDtypeStruct((MOMS, slab, 2 * N, N), BF16)
    spec = pl.BlockSpec((1, 1, 2 * N, N), lambda m, a: (m, a, 0, 0))
    return pl.pallas_call(
        turn_body,
        grid=(MOMS, slab),
        out_shape=[out, out],
        in_specs=[pl.BlockSpec((2, 1, 1, N, N), lambda m, a: (0, m, a, 0, 0))],
        out_specs=[spec, spec],
        **params(1 << 20, 8 << 20),
    )(elementals)


def first_body(count, *refs):
    perams, (high_hbm, low_hbm, send_hbm), refs = refs[:count], refs[count : count + 3], refs[count + 3 :]
    wh_ref, wl_ref, high_ref, low_ref, send_ref, in_sems, out_sems = refs
    slab = high_ref.shape[1]

    def loads(mom, a):
        return [
            pltpu.make_async_copy(src.at[mom, a], dst.at[mom, a], in_sems.at[which, mom, a])
            for which, (src, dst) in enumerate(((high_hbm, high_ref), (low_hbm, low_ref)))
        ]

    def store(mom, index):
        rows = pl.ds((mom * count + index) * 32, 32)
        return pltpu.make_async_copy(
            send_ref.at[mom, index], send_hbm.at[:, rows, :], out_sems.at[mom, index]
        )

    for mom in range(MOMS):
        for a in range(slab):
            for copy in loads(mom, a):
                copy.start()
    for index, ref in enumerate(perams):
        for time in range(TIMES):
            re = ref[2 * time]
            im = ref[2 * time + 1]
            for comp, left, right in ((0, re, -im), (1, im, re)):
                row = ((index * TIMES + time) * 2 + comp) * ROWS
                for col, part in ((0, left), (N, right)):
                    high, low = halves(part)
                    wh_ref[row : row + ROWS, col : col + N] = high
                    wl_ref[row : row + ROWS, col : col + N] = low

    left = jnp.concatenate([wh_ref[...], wh_ref[...], wl_ref[...]], axis=1)
    for mom in range(MOMS):
        for pair in range(0, slab, 2):
            products = []
            for a in (pair, pair + 1):
                for copy in loads(mom, a):
                    copy.wait()
                high, low = high_ref[mom, a], low_ref[mom, a]
                products.append(dot(left, jnp.concatenate([high, low, high], axis=0)))
            for a, product in zip((pair, pair + 1), products):
                for index in range(count):
                    flat = send_ref.at[mom, index].reshape(64 * 32, 128)
                    for time in range(TIMES):
                        for comp in range(2):
                            row = ((index * TIMES + time) * 2 + comp) * ROWS
                            for half in range(2):
                                start = (time * 2 + half) * 8 + comp * 4 + a
                                flat[pl.ds(start, ROWS, stride=32), :] = product[
                                    row : row + ROWS, half * 128 : (half + 1) * 128
                                ]
        for index in range(count):
            store(mom, index).start()
    for mom in range(MOMS):
        for index in range(count):
            store(mom, index).wait()


def first(perams, high, low):
    count, slab = len(perams), high.shape[1]
    return pl.pallas_call(
        functools.partial(first_body, count),
        in_specs=[VMEM] * count + [ANY, ANY],
        out_specs=ANY,
        out_shape=jax.ShapeDtypeStruct((64, MOMS * count * 32, 128), F32),
        scratch_shapes=[pltpu.VMEM((count * 4 * ROWS, 2 * N), BF16)] * 2
        + [pltpu.VMEM((MOMS, slab, 2 * N, N), BF16)] * 2
        + [
            pltpu.VMEM((MOMS, count, 64, 32, 128), F32),
            pltpu.SemaphoreType.DMA((2, MOMS, slab)),
            pltpu.SemaphoreType.DMA((MOMS, count)),
        ],
        **params(count * 3 * 2 * 256 * 512 * 256 * 8, 6 << 20),
    )(*perams, high, low)


def weights_body(quarter_ref, own_ref, g1_ref, g2_ref, g3_ref, vh_ref, vl_ref, wh_ref, wl_ref):
    quarter = quarter_ref[0]
    nat = lax.broadcasted_iota(jnp.int32, (N, N), 0)
    col = lax.broadcasted_iota(jnp.int32, (N, N), 1)
    place = 4 * (col & 63) + (quarter ^ (col >> 6))
    order = (nat == place).astype(F32).astype(BF16)
    row = lax.broadcasted_iota(jnp.int32, (2 * N, 2 * N), 0)
    col = lax.broadcasted_iota(jnp.int32, (2 * N, 2 * N), 1)
    place = N * ((col >> 2) & 1) + 4 * (col >> 3) + (col & 3)
    spread = (row == place).astype(F32).astype(BF16)
    for time in range(TIMES):
        parts = []
        for comp in range(2):
            index = 2 * time + comp
            stacked = jnp.concatenate(
                [ref[index] for ref in (own_ref, g1_ref, g2_ref, g3_ref)], axis=0
            )
            parts.append([dot(order, part) for part in halves(stacked)])
        for which, v_ref, w_ref in ((0, vh_ref, wh_ref), (1, vl_ref, wl_ref)):
            re = parts[0][which]
            im = parts[1][which]
            re_t = re.T.astype(BF16)
            im_t = im.T
            v_ref[time, :N, :N] = re_t
            v_ref[time, :N, N:] = im_t.astype(BF16)
            v_ref[time, N:, :N] = (-im_t).astype(BF16)
            v_ref[time, N:, N:] = re_t
            re = re.astype(BF16)
            minus = (-im).astype(BF16)
            im = im.astype(BF16)
            w_ref[time, :N] = (dot(re, spread[:N]) + dot(minus, spread[N:])).astype(BF16)
            w_ref[time, N:] = (dot(im, spread[:N]) + dot(re, spread[N:])).astype(BF16)


def weights(quarter, pieces):
    return pl.pallas_call(
        weights_body,
        in_specs=[SMEM] + [VMEM] * 4,
        out_specs=[VMEM] * 4,
        out_shape=[jax.ShapeDtypeStruct((TIMES, 2 * N, 2 * N), BF16)] * 4,
        **params(2 * 2 * 2 * 2 * 256 * 512 * 512, 5 << 20),
    )(quarter, *pieces)


def last_body(with_sums, row_ref, pair_ref, *refs):
    del row_ref, pair_ref
    gots, refs = refs[:MOMS], refs[MOMS:]
    vh_ref, vl_ref, wh_ref, wl_ref = refs[:4]
    out_ref = refs[-2] if with_sums else refs[-1]
    left = jnp.concatenate([wh_ref[0], wh_ref[0], wl_ref[0]], axis=1)
    seconds = []
    for got_ref in gots:
        got = jnp.concatenate(
            [got_ref[:, half * 8 : (half + 1) * 8, :].reshape(512, 128) for half in range(2)],
            axis=1,
        )
        high, low = halves(got)
        seconds.append(dot(left, jnp.concatenate([high, low, high], axis=0)))
    rows = []
    for second in seconds:
        high, low = [jnp.concatenate([part[:N], part[N:]], axis=1) for part in halves(second)]
        rows.append(jnp.concatenate([high, high, low], axis=1))
    left = jnp.concatenate(rows, axis=0)
    fulls = []
    for comp in range(2):
        cols = slice(comp * N, (comp + 1) * N)
        right = [vh_ref[0, :, cols], vl_ref[0, :, cols], vh_ref[0, :, cols]]
        fulls.append(dot(left, jnp.concatenate(right, axis=0)))
    for mom in range(MOMS):
        for comp in range(2):
            out_ref[comp, mom, 0, 0] = fulls[comp][mom * N : (mom + 1) * N].astype(BF16)
    if not with_sums:
        return
    elems, (sums_ref, _, _, total_ref) = refs[4 : 4 + 2 * MOMS], refs[4 + 2 * MOMS :]
    time, which = pl.program_id(0), pl.program_id(1)

    @pl.when((time == 0) & (which == 0))
    def _():
        total_ref[...] = sums_ref[...]

    lane = lax.broadcasted_iota(jnp.int32, (64, 128), 1)
    total = total_ref[...]
    for mom in range(MOMS):
        high_ref, low_ref = elems[mom], elems[MOMS + mom]
        sink = high_ref[0, 0].astype(F32) + low_ref[0, 0].astype(F32)
        sink_re, sink_im = sink[:N], sink[N:]
        re, im = [full[mom * N : (mom + 1) * N] for full in fulls]
        real = jnp.sum(sink_re * re + sink_im * im)
        imag = jnp.sum(sink_re * im - sink_im * re)
        index = mom * TIMES + time
        total += jnp.where(lane == index, real, 0.0) + jnp.where(lane == index + 4, imag, 0.0)
    total_ref[...] = total


def specs(count):
    table = pl.BlockSpec((1, 2 * N, 2 * N), lambda t, w, m, rows, pair: (t, 0, 0))
    elem = pl.BlockSpec((1, 1, 2 * N, N), lambda t, w, m, rows, pair: (pair[m], rows[w], 0, 0))
    block = pl.BlockSpec(
        (64, 16, 128), lambda t, w, m, rows, pair: (0, (m * count + w) * TIMES + t, 0)
    )
    return [table] * 4, [elem] * 2, block


def last(rows, pairing, got, tables, high, low, sums, out):
    count = rows.shape[0]
    table = pl.BlockSpec((1, 2 * N, 2 * N), lambda t, w, rows, pair: (t, 0, 0))
    whole = pl.BlockSpec((64, 128), lambda t, w, rows, pair: (0, 0))
    blocks = [
        pl.BlockSpec((64, 16, 128), lambda t, w, rows, pair, m=m: (0, (m * count + w) * TIMES + t, 0))
        for m in range(MOMS)
    ]
    elems = [
        pl.BlockSpec((1, 1, 2 * N, N), lambda t, w, rows, pair, m=m: (pair[m], rows[w], 0, 0))
        for m in range(MOMS)
    ]
    with_sums = sums is not None
    extra = (*[high] * MOMS, *[low] * MOMS, sums) if with_sums else ()
    result = pl.pallas_call(
        functools.partial(last_body, with_sums),
        grid_spec=pltpu.PrefetchScalarGridSpec(
            num_scalar_prefetch=2,
            grid=(TIMES, count),
            in_specs=blocks + [table] * 4 + (elems + elems + [whole] if with_sums else []) + [ANY],
            out_specs=[
                pl.BlockSpec(
                    (2, MOMS, 1, 1, N, N), lambda t, w, rows, pair: (0, 0, t, rows[w], 0, 0)
                )
            ]
            + ([whole] if with_sums else []),
        ),
        out_shape=[jax.ShapeDtypeStruct(out.shape, BF16)]
        + ([jax.ShapeDtypeStruct((64, 128), F32)] if with_sums else []),
        input_output_aliases={2 + MOMS + 4 + len(extra): 0},
        **params(count * 3 * 2 * 2 * 512 * 512 * 256 * 4, count * (10 << 20)),
    )(rows, pairing, *[got] * MOMS, *tables, *extra, out)
    return result if with_sums else (result[0], None)


def dual_body(rows_ref, pair_ref, vh_ref, vl_ref, wh_ref, wl_ref, high_ref, low_ref, out_ref):
    del rows_ref, pair_ref
    high, low = [
        jnp.concatenate([ref[0, 0, :N], ref[0, 0, N:]], axis=1) for ref in (high_ref, low_ref)
    ]
    left = jnp.concatenate([high, high, low], axis=1)
    second = []
    for comp in range(2):
        rows = slice(comp * N, (comp + 1) * N)
        right = jnp.concatenate([vh_ref[0, rows], vl_ref[0, rows], vh_ref[0, rows]], axis=1)
        second.append(
            lax.dot_general(left, right, (((1,), (1,)), ((), ())), preferred_element_type=F32)
        )
    high, low = halves(jnp.concatenate(second, axis=0))
    right = jnp.concatenate([high, low, high], axis=0)
    for part in range(2):
        cols = slice(part * N, (part + 1) * N)
        left = jnp.concatenate([wh_ref[0, :, cols], wh_ref[0, :, cols], wl_ref[0, :, cols]], axis=0)
        full = lax.dot_general(left, right, (((0,), (0,)), ((), ())), preferred_element_type=F32)
        for half in range(2):
            out_ref[part * 32 : (part + 1) * 32, half * 8 : (half + 1) * 8, :] = full[
                :, half * 128 : (half + 1) * 128
            ].reshape(32, 8, 128)


def dual(rows, pairing, tables, high, low):
    count = rows.shape[0]
    table, elem, block = specs(count)
    return pl.pallas_call(
        dual_body,
        grid_spec=pltpu.PrefetchScalarGridSpec(
            num_scalar_prefetch=2,
            grid=(TIMES, count, MOMS),
            in_specs=table + elem,
            out_specs=block,
        ),
        out_shape=jax.ShapeDtypeStruct((64, MOMS * count * TIMES * 16, 128), F32),
        **params(count * 3 * 2 * 2 * 512 * 512 * 256 * 4, count * (8 << 20)),
    )(rows, pairing, *tables, high, low)


def meet_body(got_hbm, dual_hbm, sums_ref, total_ref, got_ref, dual_ref, sems):
    steps, share = sems.shape[1], got_ref.shape[0] // sems.shape[1]
    blocks = got_ref.shape[1] // 16
    copies = []
    for step in range(steps):
        part = pl.ds(step * share, share)
        copies.append(
            [
                pltpu.make_async_copy(src.at[part], dst.at[part], sems.at[which, step])
                for which, (src, dst) in enumerate(((got_hbm, got_ref), (dual_hbm, dual_ref)))
            ]
        )
        for copy in copies[-1]:
            copy.start()
    sums = [[jnp.zeros((8, 128), F32)] * (MOMS * TIMES) for _ in range(2)]
    for step in range(steps):
        for copy in copies[step]:
            copy.wait()
        part = slice(step * share, (step + 1) * share)
        for block in range(blocks):
            index = block // (blocks // MOMS) * TIMES + block % TIMES
            for half in range(2):
                rows = slice(block * 16 + half * 8, block * 16 + half * 8 + 8)
                got = got_ref[part, rows, :]
                other = dual_ref[part, rows, :]
                sums[0][index] += jnp.sum(got * other, axis=0)
                sums[1][index] += jnp.sum(got * pltpu.roll(other, 4, 1), axis=0)
    sign = jnp.where((lax.broadcasted_iota(jnp.int32, (8, 128), 0) & 4) == 0, -1.0, 1.0)
    lane = lax.broadcasted_iota(jnp.int32, (64, 128), 1)
    total = sums_ref[...]
    for index in range(MOMS * TIMES):
        total += jnp.where(lane == index, jnp.sum(sums[0][index]), 0.0)
        total += jnp.where(lane == index + 4, jnp.sum(sign * sums[1][index]), 0.0)
    total_ref[...] = total


def meet(got, other, sums):
    return pl.pallas_call(
        meet_body,
        in_specs=[ANY, ANY, VMEM],
        out_specs=VMEM,
        out_shape=jax.ShapeDtypeStruct((64, 128), F32),
        scratch_shapes=[pltpu.VMEM(got.shape, F32)] * 2 + [pltpu.SemaphoreType.DMA((2, 8))],
        **params(1 << 22, 8 << 20),
    )(got, other, sums)


def empty_body(out_ref):
    del out_ref


def shards(elementals, perambulators, owners, pairing):
    slab = elementals.shape[2]
    quarter = lax.axis_index("mom").astype(jnp.int32)

    mine = perambulators[0].reshape(TIMES, 2, 64, 4, N)
    mine = lax.dynamic_index_in_dim(mine, quarter, 3, keepdims=False)
    mine = mine.reshape(4, 64, N).transpose(1, 0, 2)
    pieces = lax.all_to_all(mine, "modes", 0, 0, tiled=True)
    piece = jnp.concatenate(
        [
            lax.dynamic_slice(pieces, (owners[time], 2 * time, 0), (1, 2, N))
            for time in range(TIMES)
        ],
        axis=1,
    )
    own = lax.all_to_all(jnp.broadcast_to(piece, (64, 4, N)), "modes", 0, 0, tiled=True)
    own = own.transpose(1, 0, 2)
    by_core = lax.ppermute(own, "mom", [(i ^ 1, i) for i in range(4)])
    by_chip = lax.ppermute(own, "mom", [(i ^ 2, i) for i in range(4)])
    by_both = lax.ppermute(by_chip, "mom", [(i ^ 1, i) for i in range(4)])
    quarters = [own, by_core, by_chip, by_both]

    high, low = turn(elementals)
    tables = weights(quarter[None], quarters)
    out = pl.pallas_call(
        empty_body,
        out_shape=jax.ShapeDtypeStruct((2, MOMS, TIMES, slab, N, N), BF16),
        out_specs=ANY,
    )()
    sums = jnp.zeros((64, 128), F32)
    rows = jnp.stack([quarter ^ 2, quarter ^ 3])
    other = dual(rows, pairing, tables, high, low)
    gots = []
    for name in range(2):
        sent = first(quarters[2 * name : 2 * name + 2], high, low)
        gots.append(lax.all_to_all(sent, "modes", 0, 0, tiled=True))
    near = jnp.stack([quarter, quarter ^ 1])
    out, sums = last(near, pairing, gots[0], tables, high, low, sums, out)
    sums = meet(gots[1], other, sums)
    sums = lax.all_to_all(sums, "modes", 0, 0, tiled=True)
    out, _ = last(rows, pairing, gots[1], tables, high, low, None, out)
    correlator = jnp.sum(sums[:, :8], axis=0).reshape(2, MOMS, TIMES) * float(N) ** -1.5
    return out, correlator


def solution(mesh):
    placed = (
        P(None, "mom", "modes", None, None),
        P("modes", None, None, None, None),
        P(),
        P("mom"),
    )
    return jax.shard_map(
        shards,
        mesh=mesh,
        in_specs=placed,
        out_specs=(P(None, "mom", None, "modes", None, None), P(None, "mom", None)),
        check_vma=False,
    )
```

```python
import functools

import jax
import jax.numpy as jnp
from jax import lax
from jax.experimental import pallas as pl
from jax.experimental.pallas import tpu as pltpu
from jax.sharding import PartitionSpec as P

N = 256
ROWS = 64
MOMS = 2
TIMES = 2
PITCH = 40
F32 = jnp.float32
BF16 = jnp.bfloat16
VMEM = pl.BlockSpec(memory_space=pltpu.VMEM)
SMEM = pl.BlockSpec(memory_space=pltpu.SMEM)
ANY = pl.BlockSpec(memory_space=pl.ANY)


def halves(x):
    high = x.astype(BF16)
    return high, (x - high.astype(F32)).astype(BF16)


def dot(a, b):
    return jnp.dot(a, b, preferred_element_type=F32)


def params(flops, nbytes):
    return dict(
        cost_estimate=pl.CostEstimate(flops=flops, bytes_accessed=nbytes, transcendentals=0),
    )


def turn_body(elem_ref, high_ref, low_ref):
    for comp in range(2):
        high, low = halves(elem_ref[comp, 0, 0].T)
        high_ref[0, 0, comp * N : (comp + 1) * N, :] = high
        low_ref[0, 0, comp * N : (comp + 1) * N, :] = low


def turn(elementals):
    slab = elementals.shape[2]
    out = jax.ShapeDtypeStruct((MOMS, slab, 2 * N, N), BF16)
    spec = pl.BlockSpec((1, 1, 2 * N, N), lambda m, a: (m, a, 0, 0))
    return pl.pallas_call(
        turn_body,
        grid=(MOMS, slab),
        out_shape=[out, out],
        in_specs=[pl.BlockSpec((2, 1, 1, N, N), lambda m, a: (0, m, a, 0, 0))],
        out_specs=[spec, spec],
        **params(1 << 20, 8 << 20),
    )(elementals)


def first_body(count, *refs):
    perams, (high_hbm, low_hbm, send_hbm), refs = refs[:count], refs[count : count + 3], refs[count + 3 :]
    wh_ref, wl_ref, high_ref, low_ref, send_ref, in_sems, out_sems = refs
    slab = high_ref.shape[1]

    def loads(mom, a):
        return [
            pltpu.make_async_copy(src.at[mom, a], dst.at[mom, a], in_sems.at[which, mom, a])
            for which, (src, dst) in enumerate(((high_hbm, high_ref), (low_hbm, low_ref)))
        ]

    def store(mom, index):
        rows = pl.ds((mom * count + index) * 32, 32)
        return pltpu.make_async_copy(
            send_ref.at[mom, index, :, pl.ds(0, 32), :], send_hbm.at[:, rows, :], out_sems.at[mom, index]
        )

    for mom in range(MOMS):
        for a in range(slab):
            for copy in loads(mom, a):
                copy.start()
    for index, ref in enumerate(perams):
        for time in range(TIMES):
            re = ref[2 * time]
            im = ref[2 * time + 1]
            for comp, left, right in ((0, re, -im), (1, im, re)):
                row = ((index * TIMES + time) * 2 + comp) * ROWS
                for col, part in ((0, left), (N, right)):
                    high, low = halves(part)
                    wh_ref[row : row + ROWS, col : col + N] = high
                    wl_ref[row : row + ROWS, col : col + N] = low

    flat = send_ref.reshape(MOMS * count * 64 * PITCH, 128)

    def step(turn, carry):
        mom = turn // (slab // 2)
        pair = turn % (slab // 2) * 2
        left = jnp.concatenate([wh_ref[...], wh_ref[...], wl_ref[...]], axis=1)
        products = []
        for which in range(2):
            a = pair + which
            for copy in loads(mom, a):
                copy.wait()
            high, low = high_ref[mom, a], low_ref[mom, a]
            products.append(dot(left, jnp.concatenate([high, low, high], axis=0)))
        for which, product in enumerate(products):
            for index in range(count):
                for time in range(TIMES):
                    for comp in range(2):
                        row = ((index * TIMES + time) * 2 + comp) * ROWS
                        for half in range(2):
                            start = (mom * count + index) * 64 * PITCH + (time * 2 + half) * 8
                            start += comp * 4 + pair + which
                            flat[pl.ds(start, ROWS, stride=PITCH), :] = product[
                                row : row + ROWS, half * 128 : (half + 1) * 128
                            ]

        @pl.when(pair == slab - 2)
        def _():
            for index in range(count):
                store(mom, index).start()

        return carry

    lax.fori_loop(0, MOMS * slab // 2, step, 0)
    for mom in range(MOMS):
        for index in range(count):
            store(mom, index).wait()


def first(perams, high, low):
    count, slab = len(perams), high.shape[1]
    return pl.pallas_call(
        functools.partial(first_body, count),
        in_specs=[VMEM] * count + [ANY, ANY],
        out_specs=ANY,
        out_shape=jax.ShapeDtypeStruct((64, MOMS * count * 32, 128), F32),
        scratch_shapes=[pltpu.VMEM((count * 4 * ROWS, 2 * N), BF16)] * 2
        + [pltpu.VMEM((MOMS, slab, 2 * N, N), BF16)] * 2
        + [
            pltpu.VMEM((MOMS, count, 64, PITCH, 128), F32),
            pltpu.SemaphoreType.DMA((2, MOMS, slab)),
            pltpu.SemaphoreType.DMA((MOMS, count)),
        ],
        **params(count * 3 * 2 * 256 * 512 * 256 * 8, 6 << 20),
    )(*perams, high, low)


def weights_body(quarter_ref, own_ref, g1_ref, g2_ref, g3_ref, vh_ref, vl_ref, wh_ref, wl_ref):
    quarter = quarter_ref[0]
    nat = lax.broadcasted_iota(jnp.int32, (N, N), 0)
    col = lax.broadcasted_iota(jnp.int32, (N, N), 1)
    place = 4 * (col & 63) + (quarter ^ (col >> 6))
    order = (nat == place).astype(F32).astype(BF16)
    row = lax.broadcasted_iota(jnp.int32, (2 * N, 2 * N), 0)
    col = lax.broadcasted_iota(jnp.int32, (2 * N, 2 * N), 1)
    place = N * ((col >> 2) & 1) + 4 * (col >> 3) + (col & 3)
    spread = (row == place).astype(F32).astype(BF16)
    for time in range(TIMES):
        parts = []
        for comp in range(2):
            index = 2 * time + comp
            stacked = jnp.concatenate(
                [ref[index] for ref in (own_ref, g1_ref, g2_ref, g3_ref)], axis=0
            )
            parts.append([dot(order, part) for part in halves(stacked)])
        for which, v_ref, w_ref in ((0, vh_ref, wh_ref), (1, vl_ref, wl_ref)):
            re = parts[0][which]
            im = parts[1][which]
            re_t = re.T.astype(BF16)
            im_t = im.T
            v_ref[time, :N, :N] = re_t
            v_ref[time, :N, N:] = im_t.astype(BF16)
            v_ref[time, N:, :N] = (-im_t).astype(BF16)
            v_ref[time, N:, N:] = re_t
            re = re.astype(BF16)
            minus = (-im).astype(BF16)
            im = im.astype(BF16)
            w_ref[time, :N] = (dot(re, spread[:N]) + dot(minus, spread[N:])).astype(BF16)
            w_ref[time, N:] = (dot(im, spread[:N]) + dot(re, spread[N:])).astype(BF16)


def weights(quarter, pieces):
    return pl.pallas_call(
        weights_body,
        in_specs=[SMEM] + [VMEM] * 4,
        out_specs=[VMEM] * 4,
        out_shape=[jax.ShapeDtypeStruct((TIMES, 2 * N, 2 * N), BF16)] * 4,
        **params(2 * 2 * 2 * 2 * 256 * 512 * 512, 5 << 20),
    )(quarter, *pieces)


def last_body(with_sums, row_ref, pair_ref, *refs):
    del row_ref, pair_ref
    gots, refs = refs[:MOMS], refs[MOMS:]
    vh_ref, vl_ref, wh_ref, wl_ref = refs[:4]
    out_ref = refs[-2] if with_sums else refs[-1]
    left = jnp.concatenate([wh_ref[0], wh_ref[0], wl_ref[0]], axis=1)
    seconds = []
    for got_ref in gots:
        got = jnp.concatenate(
            [got_ref[:, half * 8 : (half + 1) * 8, :].reshape(512, 128) for half in range(2)],
            axis=1,
        )
        high, low = halves(got)
        seconds.append(dot(left, jnp.concatenate([high, low, high], axis=0)))
    rows = []
    for second in seconds:
        high, low = [jnp.concatenate([part[:N], part[N:]], axis=1) for part in halves(second)]
        rows.append(jnp.concatenate([high, high, low], axis=1))
    left = jnp.concatenate(rows, axis=0)
    fulls = []
    for comp in range(2):
        cols = slice(comp * N, (comp + 1) * N)
        right = [vh_ref[0, :, cols], vl_ref[0, :, cols], vh_ref[0, :, cols]]
        fulls.append(dot(left, jnp.concatenate(right, axis=0)))
    for mom in range(MOMS):
        for comp in range(2):
            out_ref[comp, mom, 0, 0] = fulls[comp][mom * N : (mom + 1) * N].astype(BF16)
    if not with_sums:
        return
    elems, (sums_ref, _, _, total_ref) = refs[4 : 4 + 2 * MOMS], refs[4 + 2 * MOMS :]
    time, which = pl.program_id(0), pl.program_id(1)

    @pl.when((time == 0) & (which == 0))
    def _():
        total_ref[...] = sums_ref[...]

    lane = lax.broadcasted_iota(jnp.int32, (64, 128), 1)
    total = total_ref[...]
    for mom in range(MOMS):
        high_ref, low_ref = elems[mom], elems[MOMS + mom]
        sink = high_ref[0, 0].astype(F32) + low_ref[0, 0].astype(F32)
        sink_re, sink_im = sink[:N], sink[N:]
        re, im = [full[mom * N : (mom + 1) * N] for full in fulls]
        real = jnp.sum(sink_re * re + sink_im * im)
        imag = jnp.sum(sink_re * im - sink_im * re)
        index = mom * TIMES + time
        total += jnp.where(lane == index, real, 0.0) + jnp.where(lane == index + 4, imag, 0.0)
    total_ref[...] = total


def specs(count):
    table = pl.BlockSpec((1, 2 * N, 2 * N), lambda t, w, m, rows, pair: (t, 0, 0))
    elem = pl.BlockSpec((1, 1, 2 * N, N), lambda t, w, m, rows, pair: (pair[m], rows[w], 0, 0))
    block = pl.BlockSpec(
        (64, 16, 128), lambda t, w, m, rows, pair: (0, (m * count + w) * TIMES + t, 0)
    )
    return [table] * 4, [elem] * 2, block


def last(rows, pairing, got, tables, high, low, sums, out):
    count = rows.shape[0]
    table = pl.BlockSpec((1, 2 * N, 2 * N), lambda t, w, rows, pair: (t, 0, 0))
    whole = pl.BlockSpec((64, 128), lambda t, w, rows, pair: (0, 0))
    blocks = [
        pl.BlockSpec((64, 16, 128), lambda t, w, rows, pair, m=m: (0, (m * count + w) * TIMES + t, 0))
        for m in range(MOMS)
    ]
    elems = [
        pl.BlockSpec((1, 1, 2 * N, N), lambda t, w, rows, pair, m=m: (pair[m], rows[w], 0, 0))
        for m in range(MOMS)
    ]
    with_sums = sums is not None
    extra = (*[high] * MOMS, *[low] * MOMS, sums) if with_sums else ()
    result = pl.pallas_call(
        functools.partial(last_body, with_sums),
        grid_spec=pltpu.PrefetchScalarGridSpec(
            num_scalar_prefetch=2,
            grid=(TIMES, count),
            in_specs=blocks + [table] * 4 + (elems + elems + [whole] if with_sums else []) + [ANY],
            out_specs=[
                pl.BlockSpec(
                    (2, MOMS, 1, 1, N, N), lambda t, w, rows, pair: (0, 0, t, rows[w], 0, 0)
                )
            ]
            + ([whole] if with_sums else []),
        ),
        out_shape=[jax.ShapeDtypeStruct(out.shape, BF16)]
        + ([jax.ShapeDtypeStruct((64, 128), F32)] if with_sums else []),
        input_output_aliases={2 + MOMS + 4 + len(extra): 0},
        **params(count * 3 * 2 * 2 * 512 * 512 * 256 * 4, count * (10 << 20)),
    )(rows, pairing, *[got] * MOMS, *tables, *extra, out)
    return result if with_sums else (result[0], None)


def dual_body(rows_ref, pair_ref, vh_ref, vl_ref, wh_ref, wl_ref, high_ref, low_ref, out_ref):
    del rows_ref, pair_ref
    high, low = [
        jnp.concatenate([ref[0, 0, :N], ref[0, 0, N:]], axis=1) for ref in (high_ref, low_ref)
    ]
    left = jnp.concatenate([high, high, low], axis=1)
    second = []
    for comp in range(2):
        rows = slice(comp * N, (comp + 1) * N)
        right = jnp.concatenate([vh_ref[0, rows], vl_ref[0, rows], vh_ref[0, rows]], axis=1)
        second.append(
            lax.dot_general(left, right, (((1,), (1,)), ((), ())), preferred_element_type=F32)
        )
    high, low = halves(jnp.concatenate(second, axis=0))
    right = jnp.concatenate([high, low, high], axis=0)
    for part in range(2):
        cols = slice(part * N, (part + 1) * N)
        left = jnp.concatenate([wh_ref[0, :, cols], wh_ref[0, :, cols], wl_ref[0, :, cols]], axis=0)
        full = lax.dot_general(left, right, (((0,), (0,)), ((), ())), preferred_element_type=F32)
        for half in range(2):
            out_ref[part * 32 : (part + 1) * 32, half * 8 : (half + 1) * 8, :] = full[
                :, half * 128 : (half + 1) * 128
            ].reshape(32, 8, 128)


def dual(rows, pairing, tables, high, low):
    count = rows.shape[0]
    table, elem, block = specs(count)
    return pl.pallas_call(
        dual_body,
        grid_spec=pltpu.PrefetchScalarGridSpec(
            num_scalar_prefetch=2,
            grid=(TIMES, count, MOMS),
            in_specs=table + elem,
            out_specs=block,
        ),
        out_shape=jax.ShapeDtypeStruct((64, MOMS * count * TIMES * 16, 128), F32),
        **params(count * 3 * 2 * 2 * 512 * 512 * 256 * 4, count * (8 << 20)),
    )(rows, pairing, *tables, high, low)


def meet_body(got_hbm, dual_hbm, sums_ref, total_ref, got_ref, dual_ref, sems):
    steps, share = sems.shape[1], got_ref.shape[0] // sems.shape[1]
    blocks = got_ref.shape[1] // 16
    copies = []
    for step in range(steps):
        part = pl.ds(step * share, share)
        copies.append(
            [
                pltpu.make_async_copy(src.at[part], dst.at[part], sems.at[which, step])
                for which, (src, dst) in enumerate(((got_hbm, got_ref), (dual_hbm, dual_ref)))
            ]
        )
        for copy in copies[-1]:
            copy.start()
    sums = [[jnp.zeros((8, 128), F32)] * (MOMS * TIMES) for _ in range(2)]
    for step in range(steps):
        for copy in copies[step]:
            copy.wait()
        part = slice(step * share, (step + 1) * share)
        for block in range(blocks):
            index = block // (blocks // MOMS) * TIMES + block % TIMES
            for half in range(2):
                rows = slice(block * 16 + half * 8, block * 16 + half * 8 + 8)
                got = got_ref[part, rows, :]
                other = dual_ref[part, rows, :]
                sums[0][index] += jnp.sum(got * other, axis=0)
                sums[1][index] += jnp.sum(got * pltpu.roll(other, 4, 1), axis=0)
    sign = jnp.where((lax.broadcasted_iota(jnp.int32, (8, 128), 0) & 4) == 0, -1.0, 1.0)
    lane = lax.broadcasted_iota(jnp.int32, (64, 128), 1)
    total = sums_ref[...]
    for index in range(MOMS * TIMES):
        total += jnp.where(lane == index, jnp.sum(sums[0][index]), 0.0)
        total += jnp.where(lane == index + 4, jnp.sum(sign * sums[1][index]), 0.0)
    total_ref[...] = total


def meet(got, other, sums):
    return pl.pallas_call(
        meet_body,
        in_specs=[ANY, ANY, VMEM],
        out_specs=VMEM,
        out_shape=jax.ShapeDtypeStruct((64, 128), F32),
        scratch_shapes=[pltpu.VMEM(got.shape, F32)] * 2 + [pltpu.SemaphoreType.DMA((2, 8))],
        **params(1 << 22, 8 << 20),
    )(got, other, sums)


def empty_body(out_ref):
    del out_ref


def shards(elementals, perambulators, owners, pairing):
    slab = elementals.shape[2]
    quarter = lax.axis_index("mom").astype(jnp.int32)

    mine = perambulators[0].reshape(TIMES, 2, 64, 4, N)
    mine = lax.dynamic_index_in_dim(mine, quarter, 3, keepdims=False)
    mine = mine.reshape(4, 64, N).transpose(1, 0, 2)
    pieces = lax.all_to_all(mine, "modes", 0, 0, tiled=True)
    piece = jnp.concatenate(
        [
            lax.dynamic_slice(pieces, (owners[time], 2 * time, 0), (1, 2, N))
            for time in range(TIMES)
        ],
        axis=1,
    )
    own = lax.all_to_all(jnp.broadcast_to(piece, (64, 4, N)), "modes", 0, 0, tiled=True)
    own = own.transpose(1, 0, 2)
    by_core = lax.ppermute(own, "mom", [(i ^ 1, i) for i in range(4)])
    by_chip = lax.ppermute(own, "mom", [(i ^ 2, i) for i in range(4)])
    by_both = lax.ppermute(by_chip, "mom", [(i ^ 1, i) for i in range(4)])
    quarters = [own, by_core, by_chip, by_both]

    high, low = turn(elementals)
    tables = weights(quarter[None], quarters)
    out = pl.pallas_call(
        empty_body,
        out_shape=jax.ShapeDtypeStruct((2, MOMS, TIMES, slab, N, N), BF16),
        out_specs=ANY,
    )()
    sums = jnp.zeros((64, 128), F32)
    rows = jnp.stack([quarter ^ 2, quarter ^ 3])
    other = dual(rows, pairing, tables, high, low)
    gots = []
    for name in range(2):
        sent = first(quarters[2 * name : 2 * name + 2], high, low)
        gots.append(lax.all_to_all(sent, "modes", 0, 0, tiled=True))
    near = jnp.stack([quarter, quarter ^ 1])
    out, sums = last(near, pairing, gots[0], tables, high, low, sums, out)
    sums = meet(gots[1], other, sums)
    sums = lax.all_to_all(sums, "modes", 0, 0, tiled=True)
    out, _ = last(rows, pairing, gots[1], tables, high, low, None, out)
    correlator = jnp.sum(sums[:, :8], axis=0).reshape(2, MOMS, TIMES) * float(N) ** -1.5
    return out, correlator


def solution(mesh):
    placed = (
        P(None, "mom", "modes", None, None),
        P("modes", None, None, None, None),
        P(),
        P("mom"),
    )
    return jax.shard_map(
        shards,
        mesh=mesh,
        in_specs=placed,
        out_specs=(P(None, "mom", None, "modes", None, None), P(None, "mom", None)),
        check_vma=False,
    )
```

```python
import functools

import jax
import jax.numpy as jnp
from jax import lax
from jax.experimental import pallas as pl
from jax.experimental.pallas import tpu as pltpu
from jax.sharding import PartitionSpec as P

N = 256
ROWS = 64
MOMS = 2
TIMES = 2
PITCH = 40
F32 = jnp.float32
BF16 = jnp.bfloat16
VMEM = pl.BlockSpec(memory_space=pltpu.VMEM)
SMEM = pl.BlockSpec(memory_space=pltpu.SMEM)
ANY = pl.BlockSpec(memory_space=pl.ANY)


def halves(x):
    high = x.astype(BF16)
    return high, (x - high.astype(F32)).astype(BF16)


def dot(a, b):
    return jnp.dot(a, b, preferred_element_type=F32)


def params(flops, nbytes):
    return dict(
        cost_estimate=pl.CostEstimate(flops=flops, bytes_accessed=nbytes, transcendentals=0),
    )


def turn_body(elem_ref, high_ref, low_ref):
    for comp in range(2):
        high, low = halves(elem_ref[comp, 0, 0].T)
        high_ref[0, 0, comp * N : (comp + 1) * N, :] = high
        low_ref[0, 0, comp * N : (comp + 1) * N, :] = low


def turn(elementals):
    slab = elementals.shape[2]
    out = jax.ShapeDtypeStruct((MOMS, slab, 2 * N, N), BF16)
    spec = pl.BlockSpec((1, 1, 2 * N, N), lambda m, a: (m, a, 0, 0))
    return pl.pallas_call(
        turn_body,
        grid=(MOMS, slab),
        out_shape=[out, out],
        in_specs=[pl.BlockSpec((2, 1, 1, N, N), lambda m, a: (0, m, a, 0, 0))],
        out_specs=[spec, spec],
        **params(1 << 20, 8 << 20),
    )(elementals)


def first_body(count, *refs):
    perams, (high_hbm, low_hbm, send_hbm), refs = refs[:count], refs[count : count + 3], refs[count + 3 :]
    wh_ref, wl_ref, high_ref, low_ref, send_ref, in_sems, out_sems = refs
    slab = high_ref.shape[1]

    def loads(mom, a):
        return [
            pltpu.make_async_copy(src.at[mom, a], dst.at[mom, a], in_sems.at[which, mom, a])
            for which, (src, dst) in enumerate(((high_hbm, high_ref), (low_hbm, low_ref)))
        ]

    def store(mom, index):
        rows = pl.ds((mom * count + index) * 32, 32)
        return pltpu.make_async_copy(
            send_ref.at[mom, index, :, pl.ds(0, 32), :], send_hbm.at[:, rows, :], out_sems.at[mom, index]
        )

    order = [(mom, a) for mom in range(MOMS) for a in range(slab)]
    for place in order[:2]:
        for copy in loads(*place):
            copy.start()
    for index, ref in enumerate(perams):
        for time in range(TIMES):
            re = ref[2 * time]
            im = ref[2 * time + 1]
            for comp, left, right in ((0, re, -im), (1, im, re)):
                row = ((index * TIMES + time) * 2 + comp) * ROWS
                for col, part in ((0, left), (N, right)):
                    high, low = halves(part)
                    wh_ref[row : row + ROWS, col : col + N] = high
                    wl_ref[row : row + ROWS, col : col + N] = low

    for place in order[2:]:
        for copy in loads(*place):
            copy.start()
    flat = send_ref.reshape(MOMS * count * 64 * PITCH, 128)

    def step(turn, carry):
        mom = turn // (slab // 2)
        pair = turn % (slab // 2) * 2
        left = jnp.concatenate([wh_ref[...], wh_ref[...], wl_ref[...]], axis=1)
        products = []
        for which in range(2):
            a = pair + which
            for copy in loads(mom, a):
                copy.wait()
            high, low = high_ref[mom, a], low_ref[mom, a]
            products.append(dot(left, jnp.concatenate([high, low, high], axis=0)))
        for index in range(count):
            for which, product in enumerate(products):
                for time in range(TIMES):
                    for comp in range(2):
                        row = ((index * TIMES + time) * 2 + comp) * ROWS
                        for half in range(2):
                            start = (mom * count + index) * 64 * PITCH + (time * 2 + half) * 8
                            start += comp * 4 + pair + which
                            flat[pl.ds(start, ROWS, stride=PITCH), :] = product[
                                row : row + ROWS, half * 128 : (half + 1) * 128
                            ]

            @pl.when(pair == slab - 2)
            def _(index=index):
                store(mom, index).start()

        return carry

    lax.fori_loop(0, MOMS * slab // 2, step, 0)
    for mom in range(MOMS):
        for index in range(count):
            store(mom, index).wait()


def first(perams, high, low):
    count, slab = len(perams), high.shape[1]
    return pl.pallas_call(
        functools.partial(first_body, count),
        in_specs=[VMEM] * count + [ANY, ANY],
        out_specs=ANY,
        out_shape=jax.ShapeDtypeStruct((64, MOMS * count * 32, 128), F32),
        scratch_shapes=[pltpu.VMEM((count * 4 * ROWS, 2 * N), BF16)] * 2
        + [pltpu.VMEM((MOMS, slab, 2 * N, N), BF16)] * 2
        + [
            pltpu.VMEM((MOMS, count, 64, PITCH, 128), F32),
            pltpu.SemaphoreType.DMA((2, MOMS, slab)),
            pltpu.SemaphoreType.DMA((MOMS, count)),
        ],
        **params(count * 3 * 2 * 256 * 512 * 256 * 8, 6 << 20),
    )(*perams, high, low)


def weights_body(quarter_ref, own_ref, g1_ref, g2_ref, g3_ref, vh_ref, vl_ref, wh_ref, wl_ref):
    quarter = quarter_ref[0]
    nat = lax.broadcasted_iota(jnp.int32, (N, N), 0)
    col = lax.broadcasted_iota(jnp.int32, (N, N), 1)
    place = 4 * (col & 63) + (quarter ^ (col >> 6))
    order = (nat == place).astype(F32).astype(BF16)
    row = lax.broadcasted_iota(jnp.int32, (2 * N, 2 * N), 0)
    col = lax.broadcasted_iota(jnp.int32, (2 * N, 2 * N), 1)
    place = N * ((col >> 2) & 1) + 4 * (col >> 3) + (col & 3)
    spread = (row == place).astype(F32).astype(BF16)
    for time in range(TIMES):
        parts = []
        for comp in range(2):
            index = 2 * time + comp
            stacked = jnp.concatenate(
                [ref[index] for ref in (own_ref, g1_ref, g2_ref, g3_ref)], axis=0
            )
            parts.append([dot(order, part) for part in halves(stacked)])
        for which, v_ref, w_ref in ((0, vh_ref, wh_ref), (1, vl_ref, wl_ref)):
            re = parts[0][which]
            im = parts[1][which]
            re_t = re.T.astype(BF16)
            im_t = im.T
            v_ref[time, :N, :N] = re_t
            v_ref[time, :N, N:] = im_t.astype(BF16)
            v_ref[time, N:, :N] = (-im_t).astype(BF16)
            v_ref[time, N:, N:] = re_t
            re = re.astype(BF16)
            minus = (-im).astype(BF16)
            im = im.astype(BF16)
            w_ref[time, :N] = (dot(re, spread[:N]) + dot(minus, spread[N:])).astype(BF16)
            w_ref[time, N:] = (dot(im, spread[:N]) + dot(re, spread[N:])).astype(BF16)


def weights(quarter, pieces):
    return pl.pallas_call(
        weights_body,
        in_specs=[SMEM] + [VMEM] * 4,
        out_specs=[VMEM] * 4,
        out_shape=[jax.ShapeDtypeStruct((TIMES, 2 * N, 2 * N), BF16)] * 4,
        **params(2 * 2 * 2 * 2 * 256 * 512 * 512, 5 << 20),
    )(quarter, *pieces)


def last_body(with_sums, row_ref, pair_ref, *refs):
    del row_ref, pair_ref
    gots, refs = refs[:MOMS], refs[MOMS:]
    vh_ref, vl_ref, wh_ref, wl_ref = refs[:4]
    out_ref = refs[-2] if with_sums else refs[-1]
    left = jnp.concatenate([wh_ref[0], wh_ref[0], wl_ref[0]], axis=1)
    seconds = []
    for got_ref in gots:
        got = jnp.concatenate(
            [got_ref[:, half * 8 : (half + 1) * 8, :].reshape(512, 128) for half in range(2)],
            axis=1,
        )
        high, low = halves(got)
        seconds.append(dot(left, jnp.concatenate([high, low, high], axis=0)))
    rows = []
    for second in seconds:
        high, low = [jnp.concatenate([part[:N], part[N:]], axis=1) for part in halves(second)]
        rows.append(jnp.concatenate([high, high, low], axis=1))
    left = jnp.concatenate(rows, axis=0)
    fulls = []
    for comp in range(2):
        cols = slice(comp * N, (comp + 1) * N)
        right = [vh_ref[0, :, cols], vl_ref[0, :, cols], vh_ref[0, :, cols]]
        fulls.append(dot(left, jnp.concatenate(right, axis=0)))
    for mom in range(MOMS):
        for comp in range(2):
            out_ref[comp, mom, 0, 0] = fulls[comp][mom * N : (mom + 1) * N].astype(BF16)
    if not with_sums:
        return
    elems, (sums_ref, _, _, total_ref) = refs[4 : 4 + 2 * MOMS], refs[4 + 2 * MOMS :]
    time, which = pl.program_id(0), pl.program_id(1)

    @pl.when((time == 0) & (which == 0))
    def _():
        total_ref[...] = sums_ref[...]

    lane = lax.broadcasted_iota(jnp.int32, (64, 128), 1)
    total = total_ref[...]
    for mom in range(MOMS):
        high_ref, low_ref = elems[mom], elems[MOMS + mom]
        sink = high_ref[0, 0].astype(F32) + low_ref[0, 0].astype(F32)
        sink_re, sink_im = sink[:N], sink[N:]
        re, im = [full[mom * N : (mom + 1) * N] for full in fulls]
        real = jnp.sum(sink_re * re + sink_im * im)
        imag = jnp.sum(sink_re * im - sink_im * re)
        index = mom * TIMES + time
        total += jnp.where(lane == index, real, 0.0) + jnp.where(lane == index + 4, imag, 0.0)
    total_ref[...] = total


def specs(count):
    table = pl.BlockSpec((1, 2 * N, 2 * N), lambda t, w, m, rows, pair: (t, 0, 0))
    elem = pl.BlockSpec((1, 1, 2 * N, N), lambda t, w, m, rows, pair: (pair[m], rows[w], 0, 0))
    block = pl.BlockSpec(
        (64, 16, 128), lambda t, w, m, rows, pair: (0, (m * count + w) * TIMES + t, 0)
    )
    return [table] * 4, [elem] * 2, block


def last(rows, pairing, got, tables, high, low, sums, out):
    count = rows.shape[0]
    table = pl.BlockSpec((1, 2 * N, 2 * N), lambda t, w, rows, pair: (t, 0, 0))
    whole = pl.BlockSpec((64, 128), lambda t, w, rows, pair: (0, 0))
    blocks = [
        pl.BlockSpec((64, 16, 128), lambda t, w, rows, pair, m=m: (0, (m * count + w) * TIMES + t, 0))
        for m in range(MOMS)
    ]
    elems = [
        pl.BlockSpec((1, 1, 2 * N, N), lambda t, w, rows, pair, m=m: (pair[m], rows[w], 0, 0))
        for m in range(MOMS)
    ]
    with_sums = sums is not None
    extra = (*[high] * MOMS, *[low] * MOMS, sums) if with_sums else ()
    result = pl.pallas_call(
        functools.partial(last_body, with_sums),
        grid_spec=pltpu.PrefetchScalarGridSpec(
            num_scalar_prefetch=2,
            grid=(TIMES, count),
            in_specs=blocks + [table] * 4 + (elems + elems + [whole] if with_sums else []) + [ANY],
            out_specs=[
                pl.BlockSpec(
                    (2, MOMS, 1, 1, N, N), lambda t, w, rows, pair: (0, 0, t, rows[w], 0, 0)
                )
            ]
            + ([whole] if with_sums else []),
        ),
        out_shape=[jax.ShapeDtypeStruct(out.shape, BF16)]
        + ([jax.ShapeDtypeStruct((64, 128), F32)] if with_sums else []),
        input_output_aliases={2 + MOMS + 4 + len(extra): 0},
        **params(count * 3 * 2 * 2 * 512 * 512 * 256 * 4, count * (10 << 20)),
    )(rows, pairing, *[got] * MOMS, *tables, *extra, out)
    return result if with_sums else (result[0], None)


def dual_body(rows_ref, pair_ref, vh_ref, vl_ref, wh_ref, wl_ref, high_ref, low_ref, out_ref):
    del rows_ref, pair_ref
    high, low = [
        jnp.concatenate([ref[0, 0, :N], ref[0, 0, N:]], axis=1) for ref in (high_ref, low_ref)
    ]
    left = jnp.concatenate([high, high, low], axis=1)
    second = []
    for comp in range(2):
        rows = slice(comp * N, (comp + 1) * N)
        right = jnp.concatenate([vh_ref[0, rows], vl_ref[0, rows], vh_ref[0, rows]], axis=1)
        second.append(
            lax.dot_general(left, right, (((1,), (1,)), ((), ())), preferred_element_type=F32)
        )
    high, low = halves(jnp.concatenate(second, axis=0))
    right = jnp.concatenate([high, low, high], axis=0)
    for part in range(2):
        cols = slice(part * N, (part + 1) * N)
        left = jnp.concatenate([wh_ref[0, :, cols], wh_ref[0, :, cols], wl_ref[0, :, cols]], axis=0)
        full = lax.dot_general(left, right, (((0,), (0,)), ((), ())), preferred_element_type=F32)
        for half in range(2):
            out_ref[part * 32 : (part + 1) * 32, half * 8 : (half + 1) * 8, :] = full[
                :, half * 128 : (half + 1) * 128
            ].reshape(32, 8, 128)


def dual(rows, pairing, tables, high, low):
    count = rows.shape[0]
    table, elem, block = specs(count)
    return pl.pallas_call(
        dual_body,
        grid_spec=pltpu.PrefetchScalarGridSpec(
            num_scalar_prefetch=2,
            grid=(TIMES, count, MOMS),
            in_specs=table + elem,
            out_specs=block,
        ),
        out_shape=jax.ShapeDtypeStruct((64, MOMS * count * TIMES * 16, 128), F32),
        **params(count * 3 * 2 * 2 * 512 * 512 * 256 * 4, count * (8 << 20)),
    )(rows, pairing, *tables, high, low)


def meet_body(got_hbm, dual_hbm, sums_ref, total_ref, got_ref, dual_ref, sems):
    steps, share = sems.shape[1], got_ref.shape[0] // sems.shape[1]
    blocks = got_ref.shape[1] // 16
    copies = []
    for step in range(steps):
        part = pl.ds(step * share, share)
        copies.append(
            [
                pltpu.make_async_copy(src.at[part], dst.at[part], sems.at[which, step])
                for which, (src, dst) in enumerate(((got_hbm, got_ref), (dual_hbm, dual_ref)))
            ]
        )
        for copy in copies[-1]:
            copy.start()
    sums = [[jnp.zeros((8, 128), F32)] * (MOMS * TIMES) for _ in range(2)]
    for step in range(steps):
        for copy in copies[step]:
            copy.wait()
        part = slice(step * share, (step + 1) * share)
        for block in range(blocks):
            index = block // (blocks // MOMS) * TIMES + block % TIMES
            for half in range(2):
                rows = slice(block * 16 + half * 8, block * 16 + half * 8 + 8)
                got = got_ref[part, rows, :]
                other = dual_ref[part, rows, :]
                sums[0][index] += jnp.sum(got * other, axis=0)
                sums[1][index] += jnp.sum(got * pltpu.roll(other, 4, 1), axis=0)
    sign = jnp.where((lax.broadcasted_iota(jnp.int32, (8, 128), 0) & 4) == 0, -1.0, 1.0)
    lane = lax.broadcasted_iota(jnp.int32, (64, 128), 1)
    total = sums_ref[...]
    for index in range(MOMS * TIMES):
        total += jnp.where(lane == index, jnp.sum(sums[0][index]), 0.0)
        total += jnp.where(lane == index + 4, jnp.sum(sign * sums[1][index]), 0.0)
    total_ref[...] = total


def meet(got, other, sums):
    return pl.pallas_call(
        meet_body,
        in_specs=[ANY, ANY, VMEM],
        out_specs=VMEM,
        out_shape=jax.ShapeDtypeStruct((64, 128), F32),
        scratch_shapes=[pltpu.VMEM(got.shape, F32)] * 2 + [pltpu.SemaphoreType.DMA((2, 8))],
        **params(1 << 22, 8 << 20),
    )(got, other, sums)


def empty_body(out_ref):
    del out_ref


def shards(elementals, perambulators, owners, pairing):
    slab = elementals.shape[2]
    quarter = lax.axis_index("mom").astype(jnp.int32)

    mine = perambulators[0].reshape(TIMES, 2, 64, 4, N)
    mine = lax.dynamic_index_in_dim(mine, quarter, 3, keepdims=False)
    mine = mine.reshape(4, 64, N).transpose(1, 0, 2)
    pieces = lax.all_to_all(mine, "modes", 0, 0, tiled=True)
    piece = jnp.concatenate(
        [
            lax.dynamic_slice(pieces, (owners[time], 2 * time, 0), (1, 2, N))
            for time in range(TIMES)
        ],
        axis=1,
    )
    own = lax.all_to_all(jnp.broadcast_to(piece, (64, 4, N)), "modes", 0, 0, tiled=True)
    own = own.transpose(1, 0, 2)
    by_core = lax.ppermute(own, "mom", [(i ^ 1, i) for i in range(4)])
    by_chip = lax.ppermute(own, "mom", [(i ^ 2, i) for i in range(4)])
    by_both = lax.ppermute(by_chip, "mom", [(i ^ 1, i) for i in range(4)])
    quarters = [own, by_core, by_chip, by_both]

    high, low = turn(elementals)
    tables = weights(quarter[None], quarters)
    out = pl.pallas_call(
        empty_body,
        out_shape=jax.ShapeDtypeStruct((2, MOMS, TIMES, slab, N, N), BF16),
        out_specs=ANY,
    )()
    sums = jnp.zeros((64, 128), F32)
    rows = jnp.stack([quarter ^ 2, quarter ^ 3])
    other = dual(rows, pairing, tables, high, low)
    gots = []
    for name in range(2):
        sent = first(quarters[2 * name : 2 * name + 2], high, low)
        gots.append(lax.all_to_all(sent, "modes", 0, 0, tiled=True))
    near = jnp.stack([quarter, quarter ^ 1])
    out, sums = last(near, pairing, gots[0], tables, high, low, sums, out)
    sums = meet(gots[1], other, sums)
    sums = lax.all_to_all(sums, "modes", 0, 0, tiled=True)
    out, _ = last(rows, pairing, gots[1], tables, high, low, None, out)
    correlator = jnp.sum(sums[:, :8], axis=0).reshape(2, MOMS, TIMES) * float(N) ** -1.5
    return out, correlator


def solution(mesh):
    placed = (
        P(None, "mom", "modes", None, None),
        P("modes", None, None, None, None),
        P(),
        P("mom"),
    )
    return jax.shard_map(
        shards,
        mesh=mesh,
        in_specs=placed,
        out_specs=(P(None, "mom", None, "modes", None, None), P(None, "mom", None)),
        check_vma=False,
    )
```
